32 devices in a mesh: dp: 4 (over z), seq: 8 (over y, x, core).
Axes of the slice: x: 2, y: 2, z: 4, core: 2. Of those that a mesh axis runs over, the one named last changes fastest.
Arguments:
- tokens: bfloat16 [32, 1024, 1024], P('dp', 'seq'), may hold values from -6 to 6
- ln1_gain: bfloat16 [1024], P(('dp', 'seq')), may hold values from 0.099609375 to 1.8984375
- ln1_shift: bfloat16 [1024], P(('dp', 'seq')), may hold values from -3 to 3
- ln2_gain: bfloat16 [1024], P(('dp', 'seq')), may hold values from 0.099609375 to 1.8984375
- ln2_shift: bfloat16 [1024], P(('dp', 'seq')), may hold values from -3 to 3
- qkv_weight: bfloat16 [1024, 3072], P(('dp', 'seq')), may hold values from -0.1875 to 0.1875
- qkv_bias: bfloat16 [3072], P(('dp', 'seq')), may hold values from -0.29882812 to 0.29882812
- out_weight: bfloat16 [1024, 1024], P(('dp', 'seq')), may hold values from -1.5 to 1.5
- out_bias: bfloat16 [1024], P(('dp', 'seq')), may hold values from -3 to 3
- in_weight: bfloat16 [1024, 4096], P(('dp', 'seq')), may hold values from -0.1875 to 0.1875
- in_bias: bfloat16 [4096], P(('dp', 'seq')), may hold values from -3 to 3
- down_weight: bfloat16 [4096, 1024], P(('dp', 'seq')), may hold values from -0.09375 to 0.09375
- down_bias: bfloat16 [1024], P(('dp', 'seq')), may hold values from -3 to 3
- cotangent: bfloat16 [32, 1024, 1024], P('dp', 'seq'), may hold values from -6 to 6
Outputs:
- output: bfloat16 [32, 1024, 1024], P('dp', 'seq')
- input_grad: float32 [32, 1024, 1024], P('dp', 'seq')
- ln1_gain_grad: float32 [1024], P(('dp', 'seq'))
- ln1_shift_grad: float32 [1024], P(('dp', 'seq'))
- ln2_gain_grad: float32 [1024], P(('dp', 'seq'))
- ln2_shift_grad: float32 [1024], P(('dp', 'seq'))
- qkv_weight_grad: float32 [1024, 3072], P(('dp', 'seq'))
- qkv_bias_grad: float32 [3072], P(('dp', 'seq'))
- out_weight_grad: float32 [1024, 1024], P(('dp', 'seq'))
- out_bias_grad: float32 [1024], P(('dp', 'seq'))
- in_weight_grad: float32 [1024, 4096], P(('dp', 'seq'))
- in_bias_grad: float32 [4096], P(('dp', 'seq'))
- down_weight_grad: float32 [4096, 1024], P(('dp', 'seq'))
- down_bias_grad: float32 [1024], P(('dp', 'seq'))
The draws below stay inside these ranges and needn't reach their ends.
All inputs are finite; a program needn't handle non-finite values.
Results may differ from the reference program's by a relative error of at most 0.011.
Values may be sent and summed in bfloat16 or wider, within the bound.
No kernel may reach another device: no remote copies, remote signals or barrier semaphores. Data moves between devices by JAX's collectives and lax.ppermute only.
A program may use at most 192 MiB of HBM per device.

```python
import math
import jax
import jax.numpy as jnp
from jax import lax

D = 1024
H = 16
HD = 64
ROT = 16
FF = 4096
SEQS = 32
LEN = 1024


def raised(result, own_key, source, target, shards_of, factor):
    def block_of(position):
        return (jnp.arange(result.shape[position]) // (result.shape[position] // shards_of)).reshape((-1,) + (1,) * (result.ndim - 1 - position))

    first = jax.random.permutation(own_key, shards_of)[block_of(target)]
    other_side = (block_of(target) + shards_of // 2) % shards_of
    return jnp.where((block_of(source) == first) | (block_of(source) == other_side), factor * result, result)


def shard_levels(key, dims, split, low, top_value):
    loudness = 1.0
    for position, shards_of in split:
        heights = jax.random.uniform(jax.random.fold_in(jax.random.fold_in(key, 6), position), (shards_of,), jnp.float32, low / len(split), top_value / len(split))
        loudness = loudness * jnp.repeat(jnp.exp(heights), dims[position] // shards_of).reshape((-1,) + (1,) * (len(dims) - 1 - position))
    return loudness


def bell_draw(own_key, shape, spread, limit, split=(), held_as=jnp.bfloat16):
    factor_of = shard_levels(own_key, shape, split, -0.22, 0.18) if split else 1.0
    entries = jax.random.normal(own_key, shape, jnp.float32) * spread * factor_of
    return jnp.minimum(jnp.maximum(entries, -limit), limit).astype(held_as)


def noise_with(rng, shape, scale, bound, shards, heavy, held_as=jnp.bfloat16):
    result = scale * jax.random.normal(rng, shape, jnp.float32)
    if shards:
        result = result * shard_levels(rng, shape, shards, -0.22, 0.18)
    return jnp.clip(raised(result, jax.random.fold_in(rng, 3), *heavy), -bound, bound).astype(held_as)


def setup_inputs(seed: int = 0) -> dict:
    streams_of = jax.random.split(jax.random.key(seed), 15)
    tokens = bell_draw(streams_of[0], (SEQS, LEN, D), 1.0, 6.0, ((0, 4), (1, 8)))
    ln1_gain = jnp.clip(1.0 + 0.18 * jax.random.normal(streams_of[1], (D,), jnp.float32), 0.099609375, 1.8984375).astype(jnp.bfloat16)
    ln1_shift = bell_draw(streams_of[2], (D,), 0.5, 3.0, ((0, 32),))
    ln2_gain = jnp.clip(1.0 + 0.18 * jax.random.normal(streams_of[3], (D,), jnp.float32), 0.099609375, 1.8984375).astype(jnp.bfloat16)
    ln2_shift = bell_draw(streams_of[4], (D,), 0.5, 3.0, ((0, 32),))
    qkv_weight = bell_draw(streams_of[5], (D, 3 * D), D ** -0.5, 0.1875, ((0, 32),))
    qkv_bias = bell_draw(streams_of[6], (3 * D,), 0.05, 0.29882812, ((0, 32),))
    out_weight = bell_draw(streams_of[7], (D, D), (D // 64) ** -0.5, 1.5, ((0, 32),))
    out_bias = bell_draw(streams_of[8], (D,), 0.5, 3.0, ((0, 32),))
    in_weight = bell_draw(streams_of[9], (D, FF), D ** -0.5, 0.1875, ((0, 32),))
    in_bias = bell_draw(streams_of[10], (FF,), 0.5, 3.0, ((0, 32),))
    down_weight = bell_draw(streams_of[11], (FF, D), FF ** -0.5, 0.09375, ((0, 32),))
    down_bias = bell_draw(streams_of[12], (D,), 0.5, 3.0, ((0, 32),))
    cotangent = noise_with(streams_of[13], (SEQS, LEN, D), 1.0, 6.0, ((0, 4), (1, 8)), (1, 2, 8, 2.0))
    return {"tokens": tokens, "ln1_gain": ln1_gain, "ln1_shift": ln1_shift, "ln2_gain": ln2_gain, "ln2_shift": ln2_shift, "qkv_weight": qkv_weight, "qkv_bias": qkv_bias, "out_weight": out_weight, "out_bias": out_bias, "in_weight": in_weight, "in_bias": in_bias, "down_weight": down_weight, "down_bias": down_bias, "cotangent": cotangent}


epsilon = 1e-05

@jax.custom_vjp
def low(v):
    return lax.optimization_barrier(v.astype(jnp.bfloat16)).astype(jnp.float32)

@jax.custom_vjp
def low_back(v):
    return v

def low_keep(v):
    return (low(v), None)

def low_pass(kept, grad):
    return (grad,)

def back_keep(v):
    return (v, None)

def back_low(kept, grad):
    return (low(grad),)
low.defvjp(low_keep, low_pass)
low_back.defvjp(back_keep, back_low)

def matmul(left_side, right_side):
    return jnp.dot(left_side, right_side, precision=lax.Precision.HIGHEST, preferred_element_type=jnp.float32)

def layer_norm(features, norm_gain, norm_shift):
    average = lax.optimization_barrier(jnp.mean(features, axis=-1, keepdims=True))
    centred = features - average
    variance = lax.optimization_barrier(jnp.mean(centred * centred, axis=-1, keepdims=True))
    return centred * lax.rsqrt(variance + epsilon) * norm_gain + norm_shift

def rotary_tables(positions):
    halves = jnp.arange(ROT // 2, dtype=jnp.float32)
    inverse = jnp.exp(halves * (-2.0 * math.log(10000.0) / ROT))
    angles = positions[:, None] * inverse[None, :]
    return (jnp.cos(angles), jnp.sin(angles))

def rotate(features, cos_table, sin_table):
    middle = ROT // 2
    first_half = features[..., :middle]
    second_half = features[..., middle:ROT]
    cos_wide = cos_table[:, None, :]
    sin_wide = sin_table[:, None, :]
    return jnp.concatenate([first_half * cos_wide - second_half * sin_wide, second_half * cos_wide + first_half * sin_wide, features[..., ROT:]], axis=-1)

def head_attention(operands):
    queries, keys_in, values = operands
    length = queries.shape[1]
    factor = 1.0 / math.sqrt(HD)
    scores = low_back(jnp.einsum('gqd,gkd->gqk', queries, keys_in, precision=lax.Precision.HIGHEST) * factor)
    allowed = jnp.arange(length)[None, :] <= jnp.arange(length)[:, None]
    scores = jnp.where(allowed, scores, -1e+30)
    weights = low(jax.nn.softmax(scores, axis=-1))
    return jnp.einsum('gqk,gkd->gqd', weights, values, precision=lax.Precision.HIGHEST)

def forward(group_tokens, params):
    gain_one, shift_one, gain_two, shift_two, w_qkv, b_qkv, w_proj, b_proj, w_up, b_up, w_down, b_down = params
    groups, length, model_width = group_tokens.shape
    flat_rows = group_tokens.reshape(groups * length, model_width)
    normed_one = low(layer_norm(flat_rows, gain_one, shift_one))
    projected = low_back(matmul(normed_one, w_qkv) + b_qkv).reshape(groups, length, H, 3, HD)
    cos_table, sin_table = rotary_tables(jnp.arange(length, dtype=jnp.float32))
    queries = low_back(low(rotate(projected[:, :, :, 0], cos_table, sin_table)))
    keys_in = low_back(low(rotate(projected[:, :, :, 1], cos_table, sin_table)))
    values = low_back(low(projected[:, :, :, 2]))
    heads_first = tuple((jnp.transpose(member, (2, 0, 1, 3)) for member in (queries, keys_in, values)))
    context = lax.map(jax.checkpoint(head_attention), heads_first)
    context = low_back(low(jnp.transpose(context, (1, 2, 0, 3)).reshape(groups * length, H * HD)))
    attended = matmul(context, w_proj) + b_proj
    normed_two = low(layer_norm(flat_rows, gain_two, shift_two))
    hidden = low_back(matmul(normed_two, w_up) + b_up)
    activated = low(jax.nn.gelu(hidden, approximate=False))
    mlp_out = matmul(activated, w_down) + b_down
    return (flat_rows + attended + mlp_out).reshape(groups, length, model_width)

def reference(tokens, ln1_gain, ln1_shift, ln2_gain, ln2_shift, qkv_weight, qkv_bias, out_weight, out_bias, in_weight, in_bias, down_weight, down_bias, cotangent):
    params = tuple((member.astype(jnp.float32) for member in (ln1_gain, ln1_shift, ln2_gain, ln2_shift, qkv_weight, qkv_bias, out_weight, out_bias, in_weight, in_bias, down_weight, down_bias)))
    per_group = math.gcd(SEQS, max(1, 4096 // LEN))
    token_groups = tokens.astype(jnp.float32).reshape(SEQS // per_group, per_group, LEN, D)
    cot_groups = cotangent.astype(jnp.float32).reshape(SEQS // per_group, per_group, LEN, D)

    def group_step(running, operands):
        group_tokens, group_cot = operands
        group_out, pullback = jax.vjp(forward, group_tokens, params)
        token_grad, param_grads = pullback(group_cot)
        running = jax.tree.map(jnp.add, running, param_grads)
        return (running, (group_out.astype(jnp.bfloat16), token_grad))
    initial = tuple((jnp.zeros_like(member) for member in params))
    sums, (outputs, token_grads) = lax.scan(group_step, initial, (token_groups, cot_groups))
    return (outputs.reshape(SEQS, LEN, D), token_grads.reshape(SEQS, LEN, D), sums[0], sums[1], sums[2], sums[3], sums[4], sums[5], sums[6], sums[7], sums[8], sums[9], sums[10], sums[11])
```

```python
import functools
import math

import jax
import jax.numpy as jnp
from jax import lax
from jax.experimental import pallas as pl
from jax.experimental.pallas import tpu as pltpu
from jax.sharding import Mesh
from jax.sharding import PartitionSpec as P

H = 16
HD = 64
ROT = 16
PAIR = 2 * HD
AXES = ("dp", "pl", "core")
CHIPS = ("dp", "pl")
BF = jnp.bfloat16
F32 = jnp.float32

epsilon = 1e-05


def dot_nn(left, right):
    return lax.dot_general(left, right, (((1,), (0,)), ((), ())), preferred_element_type=F32)


def dot_nt(left, right):
    return lax.dot_general(left, right, (((1,), (1,)), ((), ())), preferred_element_type=F32)


def dot_tn(left, right):
    return lax.dot_general(left, right, (((0,), (0,)), ((), ())), preferred_element_type=F32)


def rotary_lanes(length):
    lane = jnp.arange(PAIR, dtype=jnp.int32) % HD
    half = ROT // 2
    inverse = jnp.exp((lane % half).astype(F32) * (-2.0 * math.log(10000.0) / ROT))
    angles = jnp.arange(length, dtype=F32)[:, None] * inverse[None, :]
    turned = (lane < ROT)[None, :]
    first = (lane < half)[None, :]
    sines = jnp.sin(angles)
    return (
        jnp.where(turned, jnp.cos(angles), 1.0),
        jnp.where(first, -sines, 0.0),
        jnp.where(turned & ~first, sines, 0.0),
    )


def attention_kernel(
    block,
    qkv_ref,
    dc_ref,
    cos_ref,
    sin_a_ref,
    sin_b_ref,
    ctx_ref,
    dqkv_ref,
    q_s,
    k_s,
    km_s,
    vm_s,
    ctx_s,
    dq_s,
    dk_s,
    dv_s,
):
    length = qkv_ref.shape[1]
    half = ROT // 2
    factor = 1.0 / math.sqrt(HD)

    def turn(z, sign):
        swapped = pltpu.roll(z, PAIR - half, 1) * sin_a_ref[...] + pltpu.roll(z, half, 1) * sin_b_ref[...]
        return z * cos_ref[...] + sign * swapped

    q_s[...] = turn(qkv_ref[0, :, 0:PAIR].astype(F32), 1.0).astype(BF) * BF(factor)
    k_s[...] = turn(qkv_ref[0, :, PAIR : 2 * PAIR].astype(F32), 1.0).astype(BF)
    ctx_s[...] = jnp.zeros_like(ctx_s)
    dq_s[...] = jnp.zeros_like(dq_s)
    dk_s[...] = jnp.zeros_like(dk_s)
    dv_s[...] = jnp.zeros_like(dv_s)
    lane = lax.broadcasted_iota(jnp.int32, (1, PAIR), 1)

    def one_head(head, carry):
        chosen = ((lane >= head * HD) & (lane < head * HD + HD)).astype(BF)
        km_s[...] = k_s[...] * chosen
        vm_s[...] = qkv_ref[0, :, 2 * PAIR : 3 * PAIR] * chosen
        for i in range(length // block):
            lo, hi = i * block, (i + 1) * block
            queries = q_s[lo:hi, :] * chosen
            grads = dc_ref[0, lo:hi, :] * chosen
            scores = dot_nt(km_s[0:hi, :], queries)
            keys_at = lax.broadcasted_iota(jnp.int32, (block, block), 0)
            queries_at = lax.broadcasted_iota(jnp.int32, (block, block), 1)
            last = jnp.where(keys_at <= queries_at, scores[lo:hi, :], -1e30)
            scores = jnp.concatenate([scores[:lo, :], last], 0) if i else last
            highest = jnp.max(scores, axis=0, keepdims=True)
            weights = jnp.exp(scores - highest)
            weights = weights * (1.0 / jnp.sum(weights, axis=0, keepdims=True))
            low = weights.astype(BF)
            weight_grad = dot_nt(vm_s[0:hi, :], grads)
            mixed = jnp.sum(weights * weight_grad, axis=0, keepdims=True)
            score_grad = (weights * (weight_grad - mixed)).astype(BF)
            ctx_s[lo:hi, :] += dot_tn(low, vm_s[0:hi, :])
            dv_s[0:hi, :] += dot_nn(low, grads)
            dk_s[0:hi, :] += dot_nn(score_grad, queries)
            dq_s[lo:hi, :] += dot_tn(score_grad, km_s[0:hi, :])
        return carry

    lax.fori_loop(0, 2, one_head, 0)
    ctx_ref[0] = ctx_s[...].astype(BF)
    dqkv_ref[0, :, 0:PAIR] = turn(dq_s[...] * factor, -1.0).astype(BF)
    dqkv_ref[0, :, PAIR : 2 * PAIR] = turn(dk_s[...], -1.0).astype(BF)
    dqkv_ref[0, :, 2 * PAIR : 3 * PAIR] = dv_s[...].astype(BF)


def attention(qkv, context_grad, tables):
    seqs, length, width = qkv.shape
    pairs = width // (3 * PAIR)
    table = pl.BlockSpec((length, PAIR), lambda s, h: (0, 0))
    wide = pl.BlockSpec((1, length, 3 * PAIR), lambda s, h: (s, 0, h))
    slim = pl.BlockSpec((1, length, PAIR), lambda s, h: (s, 0, h))
    return pl.pallas_call(
        functools.partial(attention_kernel, math.gcd(length, 256)),
        out_shape=(
            jax.ShapeDtypeStruct((seqs, length, width // 3), BF),
            jax.ShapeDtypeStruct((seqs, length, width), BF),
        ),
        grid=(seqs, pairs),
        in_specs=[wide, slim, table, table, table],
        out_specs=(slim, wide),
        scratch_shapes=[pltpu.VMEM((length, PAIR), BF)] * 4 + [pltpu.VMEM((length, PAIR), F32)] * 4,
        cost_estimate=pl.CostEstimate(
            flops=seqs * pairs * 2 * 7 * length * length * PAIR,
            bytes_accessed=seqs * length * width * 6,
            transcendentals=seqs * pairs * length * length,
        ),
        compiler_params=pltpu.CompilerParams(vmem_limit_bytes=60 << 20),
    )(qkv, context_grad, *tables)


def local(
    tokens,
    ln1_gain,
    ln1_shift,
    ln2_gain,
    ln2_shift,
    qkv_weight,
    qkv_bias,
    out_weight,
    out_bias,
    in_weight,
    in_bias,
    down_weight,
    down_bias,
    cotangent,
):
    planes = lax.axis_size("pl")
    chips = lax.axis_size("dp") * planes
    n = 2 * chips
    flat = (lax.axis_index("dp") * planes + lax.axis_index("pl")) * 2 + lax.axis_index("core")
    core = lax.axis_index("core")
    first_core = core == 0
    seqs, rows_here, width = tokens.shape
    per_chip = seqs // planes
    length = rows_here * planes * 2
    count = per_chip * length
    heads = H // 2
    qkv_cols = heads * 3 * HD
    ctx_cols = heads * HD
    hidden = in_weight.shape[1] // 2
    own_rows = qkv_weight.shape[0]

    def swap(value, mask):
        return lax.ppermute(value, AXES, [(i, i ^ mask) for i in range(n)])

    def in_core_order(own, other, axis):
        return jnp.where(
            first_core, jnp.concatenate([own, other], axis), jnp.concatenate([other, own], axis)
        )

    def pick(value, index, axis):
        return lax.dynamic_index_in_dim(value, index, axis, keepdims=False)

    small = jnp.concatenate(
        [ln1_gain, ln1_shift, ln2_gain, ln2_shift, out_bias, down_bias, qkv_bias, in_bias]
    )[None, :]
    for bit in range(n.bit_length() - 1):
        other = swap(small, 1 << bit)
        small = jnp.where(
            (flat >> bit) & 1 == 1,
            jnp.concatenate([other, small], 0),
            jnp.concatenate([small, other], 0),
        )
    small = small.astype(F32)
    part = width // n
    gain_one, shift_one, gain_two, shift_two, b_out, b_down = (
        small[:, i * part : (i + 1) * part].reshape(width) for i in range(6)
    )
    b_qkv = small[:, 6 * part : 9 * part].reshape(2, heads // 2, 2, 3, HD)
    b_qkv = pick(b_qkv, core, 0).transpose(0, 2, 1, 3).reshape(qkv_cols)
    b_in = pick(small[:, 9 * part :].reshape(chips, 2, hidden // chips), core, 1).reshape(hidden)

    qkv_halves = (
        qkv_weight.reshape(own_rows, 2, heads // 2, 2, 3, HD)
        .transpose(1, 0, 2, 4, 3, 5)
        .reshape(2, own_rows, qkv_cols)
    )
    out_halves = out_weight.reshape(own_rows, 2, ctx_cols).transpose(1, 0, 2)
    in_halves = (
        in_weight.reshape(own_rows, chips, 2, hidden // chips)
        .transpose(2, 0, 1, 3)
        .reshape(2, own_rows, hidden)
    )
    halves = jnp.concatenate([qkv_halves, out_halves, in_halves], 2)
    chip_rows = in_core_order(pick(halves, core, 0), swap(pick(halves, 1 - core, 0), 1), 0)
    first_cols = qkv_cols + ctx_cols
    first_all = lax.all_gather(chip_rows[:, :first_cols], CHIPS, axis=0, tiled=True)
    second = jnp.concatenate(
        [chip_rows[:, first_cols:], down_weight.reshape(2 * own_rows, hidden)], 1
    )
    second_all = lax.all_gather(second, CHIPS, axis=0, tiled=True)
    w_qkv = first_all[:, :qkv_cols]
    out_cols = first_all[:, qkv_cols:].reshape(2, ctx_cols, ctx_cols)
    w_out = in_core_order(pick(out_cols, core, 0), swap(pick(out_cols, 1 - core, 0), 1), 1)
    w_in = second_all[:, :hidden]
    w_down = second_all[:, hidden:].reshape(hidden, width)

    def to_sequences(value):
        mine = lax.all_to_all(value, "pl", split_axis=0, concat_axis=0, tiled=True)
        theirs = swap(mine, 1)
        both = in_core_order(mine[None], theirs[None], 0)
        both = both.reshape(2, planes, per_chip, rows_here, width)
        return both.transpose(2, 1, 0, 3, 4).reshape(count, width)

    def split_cores(value):
        value = value.reshape(per_chip, planes, 2, rows_here, width)
        kept = pick(value, core, 2)
        return kept + swap(pick(value, 1 - core, 2).astype(BF), 1).astype(F32)

    def to_tokens(value):
        value = value.astype(BF).transpose(1, 0, 2, 3)
        value = lax.all_to_all(value, "pl", split_axis=0, concat_axis=0, tiled=True)
        return value.reshape(seqs, rows_here, width)

    x_low = to_sequences(tokens)
    dy = to_sequences(cotangent)
    x = x_low.astype(F32)
    mean = jnp.mean(x, axis=-1, keepdims=True)
    centred = x - mean
    scale = lax.rsqrt(jnp.mean(centred * centred, axis=-1, keepdims=True) + epsilon)
    normed = centred * scale
    a_one = (normed * gain_one + shift_one).astype(BF)
    a_two = (normed * gain_two + shift_two).astype(BF)

    qkv = (dot_nn(a_one, w_qkv) + b_qkv).astype(BF)
    context_grad = dot_nt(dy, w_out).astype(BF)
    context, qkv_grad = attention(
        qkv.reshape(per_chip, length, qkv_cols),
        context_grad.reshape(per_chip, length, ctx_cols),
        rotary_lanes(length),
    )
    context = context.reshape(count, ctx_cols)
    qkv_grad = qkv_grad.reshape(count, qkv_cols)

    chip_bits = chips.bit_length() - 1
    plane_bits = planes.bit_length() - 1

    def scatter_sum(value, order):
        cols = value.shape[1]
        value = value.reshape((2,) * chip_bits + (value.shape[0] // chips, cols))
        left = list(range(chip_bits, 0, -1))
        for step, bit in enumerate(order):
            axis = left.index(bit)
            left.remove(bit)
            mine = (flat >> bit) & 1
            sent = swap(pick(value, 1 - mine, axis).astype(BF), 1 << bit)
            value = pick(value, mine, axis).astype(F32) + sent.astype(F32)
            if step < len(order) - 1:
                value = value.astype(BF)
        return value

    plane_up = list(range(1, plane_bits + 1))
    beyond = list(range(chip_bits, plane_bits, -1))
    orders = (plane_up + beyond, plane_up[::-1] + beyond)

    def scatter_two_ways(value):
        cols = value.shape[1] // 2
        return jnp.concatenate(
            [
                scatter_sum(value[:, :cols], orders[0]),
                scatter_sum(value[:, cols:], orders[1]),
            ],
            1,
        )

    def own_rows_of(value):
        value = value.reshape(2, own_rows, value.shape[1])
        return in_core_order(
            pick(value, core, 0)[:, None], swap(pick(value, 1 - core, 0), 1)[:, None], 1
        )

    qkv_w_grad = dot_tn(a_one, qkv_grad).astype(BF)
    out_w_grad = dot_tn(context, dy).astype(BF).reshape(ctx_cols, 2, ctx_cols)
    out_w_grad = in_core_order(
        pick(out_w_grad, core, 1), swap(pick(out_w_grad, 1 - core, 1), 1), 0
    )
    first_grad = own_rows_of(scatter_two_ways(jnp.concatenate([qkv_w_grad, out_w_grad], 1)))
    qkv_w_grad = (
        first_grad[:, :, :qkv_cols]
        .reshape(own_rows, 2, heads // 2, 3, 2, HD)
        .transpose(0, 1, 2, 4, 3, 5)
        .reshape(own_rows, 2 * qkv_cols)
    )
    out_w_grad = first_grad[:, :, qkv_cols:].reshape(own_rows, width)

    u = dot_nn(a_two, w_in) + b_in
    cdf = 0.5 * (1.0 + lax.erf(u * math.sqrt(0.5)))
    z = (u * cdf).astype(BF)
    slope = (cdf + u * (jnp.exp(-0.5 * u * u) * (1.0 / math.sqrt(2.0 * math.pi)))).astype(BF)
    down_w_grad = scatter_two_ways(dot_tn(z, dy).astype(BF))
    summed = split_cores(dot_nn(context, w_out) + dot_nn(z, w_down))
    own_x = pick(x_low.reshape(per_chip, planes, 2, rows_here, width), core, 2)
    output = to_tokens(own_x.astype(F32) + summed + (b_out + b_down))
    du = (dot_nt(dy, w_down) * slope.astype(F32)).astype(BF)
    in_w_grad = own_rows_of(scatter_two_ways(dot_tn(a_two, du).astype(BF)))
    in_w_grad = (
        in_w_grad.reshape(own_rows, 2, chips, hidden // chips)
        .transpose(0, 2, 1, 3)
        .reshape(own_rows, 2 * hidden)
    )
    g_two = dot_nt(du, w_in)
    g_one = dot_nt(qkv_grad, w_qkv)

    combined = to_tokens(split_cores(g_one * gain_one + g_two * gain_two))
    x_here = tokens.astype(F32)
    mean_here = jnp.mean(x_here, axis=-1, keepdims=True)
    centred_here = x_here - mean_here
    scale_here = lax.rsqrt(jnp.mean(centred_here * centred_here, axis=-1, keepdims=True) + epsilon)
    normed_here = centred_here * scale_here
    combined = combined.astype(F32)
    pulled = (
        combined
        - jnp.mean(combined, axis=-1, keepdims=True)
        - normed_here * jnp.mean(combined * normed_here, axis=-1, keepdims=True)
    ) * scale_here
    dy_here = cotangent.astype(F32)
    input_grad = dy_here + pulled

    qkv_b_grad = (
        jnp.sum(qkv_grad.astype(F32), 0)
        .reshape(heads // 2, 3, 2, HD)
        .transpose(0, 2, 1, 3)
        .reshape(qkv_cols)
    )
    nothing = jnp.zeros_like(qkv_b_grad)
    qkv_b_grad = in_core_order(qkv_b_grad, nothing, 0)
    in_b_grad = jnp.sum(du.astype(F32), 0).reshape(chips, hidden // chips)
    in_b_grad = in_core_order(in_b_grad[:, None], jnp.zeros_like(in_b_grad)[:, None], 1)
    sums = [
        jnp.sum(g_one * normed, 0),
        jnp.sum(g_one, 0),
        jnp.sum(g_two * normed, 0),
        jnp.sum(g_two, 0),
        jnp.sum(dy_here, (0, 1)),
        qkv_b_grad,
        in_b_grad,
    ]
    sums = jnp.concatenate([value.reshape(n, -1) for value in sums], 1)
    for bit in range(n.bit_length() - 2, -1, -1):
        sums = sums.reshape(2, sums.shape[0] // 2, sums.shape[1])
        mine = (flat >> bit) & 1
        sums = pick(sums, mine, 0) + swap(pick(sums, 1 - mine, 0), 1 << bit)
    sums = sums[0]
    b_grad = sums[4 * part : 5 * part]
    return (
        output,
        input_grad,
        sums[:part],
        sums[part : 2 * part],
        sums[2 * part : 3 * part],
        sums[3 * part : 4 * part],
        qkv_w_grad,
        sums[5 * part : 8 * part],
        out_w_grad,
        b_grad,
        in_w_grad,
        sums[8 * part :],
        down_w_grad,
        b_grad,
    )


def solution(mesh):
    split = Mesh(
        mesh.devices.reshape(mesh.shape["dp"], mesh.shape["seq"] // 2, 2),
        AXES,
    )
    rows = P("dp", ("pl", "core"), None)
    vector = P(AXES)
    matrix = P(AXES, None)
    return jax.shard_map(
        local,
        mesh=split,
        in_specs=(
            rows,
            vector,
            vector,
            vector,
            vector,
            matrix,
            vector,
            matrix,
            vector,
            matrix,
            vector,
            matrix,
            vector,
            rows,
        ),
        out_specs=(
            rows,
            rows,
            vector,
            vector,
            vector,
            vector,
            matrix,
            vector,
            matrix,
            vector,
            matrix,
            vector,
            matrix,
            vector,
        ),
        check_vma=False,
    )
```

```python
import functools
import math

import jax
import jax.numpy as jnp
from jax import lax
from jax.experimental import pallas as pl
from jax.experimental.pallas import tpu as pltpu
from jax.sharding import Mesh
from jax.sharding import PartitionSpec as P


H = 16
HD = 64
ROT = 16
PAIR = 2 * HD
AXES = ("dp", "pl", "core")
CHIPS = ("dp", "pl")
BF = jnp.bfloat16
F32 = jnp.float32

epsilon = 1e-05


def dot_nn(left, right):
    return lax.dot_general(left, right, (((1,), (0,)), ((), ())), preferred_element_type=F32)


def dot_nt(left, right):
    return lax.dot_general(left, right, (((1,), (1,)), ((), ())), preferred_element_type=F32)


def dot_tn(left, right):
    return lax.dot_general(left, right, (((0,), (0,)), ((), ())), preferred_element_type=F32)


def rotary_lanes(length):
    lane = jnp.arange(PAIR, dtype=jnp.int32) % HD
    half = ROT // 2
    inverse = jnp.exp((lane % half).astype(F32) * (-2.0 * math.log(10000.0) / ROT))
    angles = jnp.arange(length, dtype=F32)[:, None] * inverse[None, :]
    turned = (lane < ROT)[None, :]
    first = (lane < half)[None, :]
    sines = jnp.sin(angles)
    return (
        jnp.where(turned, jnp.cos(angles), 1.0),
        jnp.where(first, -sines, 0.0),
        jnp.where(turned & ~first, sines, 0.0),
    )


def attention_kernel(
    block,
    qkv_ref,
    dc_ref,
    cos_ref,
    sin_a_ref,
    sin_b_ref,
    ctx_ref,
    dqkv_ref,
    q_s,
    k_s,
    km_s,
    vm_s,
    ctx_s,
    dq_s,
    dk_s,
    dv_s,
):
    length = qkv_ref.shape[1]
    half = ROT // 2
    factor = 1.0 / math.sqrt(HD)

    def turn(z, sign):
        swapped = pltpu.roll(z, PAIR - half, 1) * sin_a_ref[...] + pltpu.roll(z, half, 1) * sin_b_ref[...]
        return z * cos_ref[...] + sign * swapped

    q_s[...] = turn(qkv_ref[0, :, 0:PAIR].astype(F32), 1.0).astype(BF) * BF(factor)
    k_s[...] = turn(qkv_ref[0, :, PAIR : 2 * PAIR].astype(F32), 1.0).astype(BF)
    ctx_s[...] = jnp.zeros_like(ctx_s)
    dq_s[...] = jnp.zeros_like(dq_s)
    dk_s[...] = jnp.zeros_like(dk_s)
    dv_s[...] = jnp.zeros_like(dv_s)
    lane = lax.broadcasted_iota(jnp.int32, (1, PAIR), 1)

    def one_head(head, carry):
        chosen = ((lane >= head * HD) & (lane < head * HD + HD)).astype(BF)
        km_s[...] = k_s[...] * chosen
        vm_s[...] = qkv_ref[0, :, 2 * PAIR : 3 * PAIR] * chosen
        for i in range(length // block):
            lo, hi = i * block, (i + 1) * block
            queries = q_s[lo:hi, :] * chosen
            grads = dc_ref[0, lo:hi, :] * chosen
            scores = dot_nt(km_s[0:hi, :], queries)
            keys_at = lax.broadcasted_iota(jnp.int32, (block, block), 0)
            queries_at = lax.broadcasted_iota(jnp.int32, (block, block), 1)
            last = jnp.where(keys_at <= queries_at, scores[lo:hi, :], -1e30)
            scores = jnp.concatenate([scores[:lo, :], last], 0) if i else last
            highest = jnp.max(scores, axis=0, keepdims=True)
            weights = jnp.exp(scores - highest)
            weights = weights * (1.0 / jnp.sum(weights, axis=0, keepdims=True))
            low = weights.astype(BF)
            weight_grad = dot_nt(vm_s[0:hi, :], grads)
            mixed = jnp.sum(weights * weight_grad, axis=0, keepdims=True)
            score_grad = (weights * (weight_grad - mixed)).astype(BF)
            ctx_s[lo:hi, :] += dot_tn(low, vm_s[0:hi, :])
            dv_s[0:hi, :] += dot_nn(low, grads)
            dk_s[0:hi, :] += dot_nn(score_grad, queries)
            dq_s[lo:hi, :] += dot_tn(score_grad, km_s[0:hi, :])
        return carry

    lax.fori_loop(0, 2, one_head, 0)
    ctx_ref[0] = ctx_s[...].astype(BF)
    dqkv_ref[0, :, 0:PAIR] = turn(dq_s[...] * factor, -1.0).astype(BF)
    dqkv_ref[0, :, PAIR : 2 * PAIR] = turn(dk_s[...], -1.0).astype(BF)
    dqkv_ref[0, :, 2 * PAIR : 3 * PAIR] = dv_s[...].astype(BF)


def attention(qkv, context_grad, tables):
    seqs, length, width = qkv.shape
    pairs = width // (3 * PAIR)
    table = pl.BlockSpec((length, PAIR), lambda s, h: (0, 0))
    wide = pl.BlockSpec((1, length, 3 * PAIR), lambda s, h: (s, 0, h))
    slim = pl.BlockSpec((1, length, PAIR), lambda s, h: (s, 0, h))
    return pl.pallas_call(
        functools.partial(attention_kernel, math.gcd(length, 256)),
        out_shape=(
            jax.ShapeDtypeStruct((seqs, length, width // 3), BF),
            jax.ShapeDtypeStruct((seqs, length, width), BF),
        ),
        grid=(seqs, pairs),
        in_specs=[wide, slim, table, table, table],
        out_specs=(slim, wide),
        scratch_shapes=[pltpu.VMEM((length, PAIR), BF)] * 4 + [pltpu.VMEM((length, PAIR), F32)] * 4,
        cost_estimate=pl.CostEstimate(
            flops=seqs * pairs * 2 * 7 * length * length * PAIR,
            bytes_accessed=seqs * length * width * 6,
            transcendentals=seqs * pairs * length * length,
        ),
        compiler_params=pltpu.CompilerParams(vmem_limit_bytes=60 << 20),
    )(qkv, context_grad, *tables)


def norm_kernel(core_ref, mine_ref, theirs_ref, gains_ref, one_ref, two_ref, normed_ref):
    own = pl.program_id(2) == core_ref[0]
    x = jnp.where(own, mine_ref[0].astype(F32), theirs_ref[0].astype(F32))
    centred = x - jnp.mean(x, axis=-1, keepdims=True)
    normed = centred * lax.rsqrt(jnp.mean(centred * centred, axis=-1, keepdims=True) + epsilon)
    one_ref[...] = (normed * gains_ref[0:1, :] + gains_ref[1:2, :]).astype(BF)
    two_ref[...] = (normed * gains_ref[2:3, :] + gains_ref[3:4, :]).astype(BF)
    normed_ref[...] = normed.astype(BF)


def normalize(core, mine, theirs, gains, per_chip):
    blocks, rows, width = mine.shape
    planes = blocks // per_chip
    source = pl.BlockSpec((1, rows, width), lambda s, p, c, core: (p * per_chip + s, 0, 0))
    target = pl.BlockSpec((rows, width), lambda s, p, c, core: ((s * planes + p) * 2 + c, 0))
    shape = jax.ShapeDtypeStruct((2 * blocks * rows, width), BF)
    return pl.pallas_call(
        norm_kernel,
        out_shape=(shape, shape, shape),
        grid_spec=pltpu.PrefetchScalarGridSpec(
            num_scalar_prefetch=1,
            grid=(per_chip, planes, 2),
            in_specs=[source, source, pl.BlockSpec((4, width), lambda s, p, c, core: (0, 0))],
            out_specs=(target, target, target),
        ),
        cost_estimate=pl.CostEstimate(
            flops=20 * blocks * rows * width,
            bytes_accessed=20 * blocks * rows * width,
            transcendentals=0,
        ),
    )(core.reshape(1), mine, theirs, gains)


def dy_kernel(core_ref, mine_ref, theirs_ref, dy_ref):
    own = pl.program_id(2) == core_ref[0]
    dy_ref[...] = jnp.where(own, mine_ref[0].astype(F32), theirs_ref[0].astype(F32)).astype(BF)


def arrange_cotangent(core, mine, theirs, per_chip):
    blocks, rows, width = mine.shape
    planes = blocks // per_chip
    source = pl.BlockSpec((1, rows, width), lambda s, p, c, core: (p * per_chip + s, 0, 0))
    target = pl.BlockSpec((rows, width), lambda s, p, c, core: ((s * planes + p) * 2 + c, 0))
    count = 2 * blocks * rows
    return pl.pallas_call(
        dy_kernel,
        out_shape=jax.ShapeDtypeStruct((count, width), BF),
        grid_spec=pltpu.PrefetchScalarGridSpec(
            num_scalar_prefetch=1,
            grid=(per_chip, planes, 2),
            in_specs=[source, source],
            out_specs=target,
        ),
        cost_estimate=pl.CostEstimate(
            flops=count * width, bytes_accessed=6 * count * width, transcendentals=0
        ),
    )(core.reshape(1), mine, theirs)


def phi(u):
    density = jnp.exp(-0.5 * u * u) * (1.0 / math.sqrt(2.0 * math.pi))
    return 0.5 * (1.0 + lax.erf(u * math.sqrt(0.5))), density


def up_kernel(a_ref, low_ref, high_ref, bias_ref, z_ref, slope_ref):
    width = low_ref.shape[2]
    chunk = math.gcd(width, 512)
    a = a_ref[...]
    for half, w_ref in enumerate((low_ref, high_ref)):
        for start in range(0, width, chunk):
            weight = w_ref[:, :, start : start + chunk].reshape(a.shape[1], chunk)
            at = half * width + start
            u = dot_nn(a, weight) + bias_ref[:, at : at + chunk]
            cdf, density = phi(u)
            z_ref[:, at : at + chunk] = (u * cdf).astype(BF)
            slope_ref[:, at : at + chunk] = (cdf + u * density).astype(BF)


def half_specs(shared):
    chips, rows, width = shared.shape
    low = pl.BlockSpec((chips, rows // 4, width), lambda *i: (0, 0, 0))
    high = pl.BlockSpec((chips, rows // 4, width), lambda *i: (0, 1, 0))
    down = pl.BlockSpec((chips, rows // 2, width), lambda *i: (0, 1, 0))
    return low, high, down


def up_project(a, shared, bias, block):
    count, width = a.shape
    hidden = bias.shape[1]
    low, high, _ = half_specs(shared)
    wide = pl.BlockSpec((block, hidden), lambda i: (i, 0))
    shape = jax.ShapeDtypeStruct((count, hidden), BF)
    return pl.pallas_call(
        up_kernel,
        out_shape=(shape, shape),
        grid=(count // block,),
        in_specs=[
            pl.BlockSpec((block, width), lambda i: (i, 0)),
            low,
            high,
            pl.BlockSpec((1, hidden), lambda i: (0, 0)),
        ],
        out_specs=(wide, wide),
        cost_estimate=pl.CostEstimate(
            flops=2 * count * width * hidden,
            bytes_accessed=2 * (count * width + 2 * count * hidden + width * hidden),
            transcendentals=2 * count * hidden,
        ),
        compiler_params=pltpu.CompilerParams(vmem_limit_bytes=60 << 20),
    )(a, shared, shared, bias)


def dz_kernel(dy_ref, down_ref, slope_ref, du_ref, sum_ref):
    hidden = du_ref.shape[1]
    chunk = math.gcd(hidden, 512)
    width = dy_ref.shape[1]
    dy = dy_ref[...]
    _, rows, _ = down_ref.shape

    @pl.when(pl.program_id(0) == 0)
    def _():
        sum_ref[...] = jnp.zeros_like(sum_ref)

    for start in range(0, hidden, chunk):
        part = down_ref[start // rows : (start + chunk) // rows, :, :].reshape(chunk, width)
        slope = slope_ref[:, start : start + chunk].astype(F32)
        du = (dot_nt(dy, part) * slope).astype(BF)
        du_ref[:, start : start + chunk] = du
        sum_ref[:, start : start + chunk] += jnp.sum(du.astype(F32), 0, keepdims=True)


def down_pull(dy, shared, slope, block):
    count, width = dy.shape
    hidden = slope.shape[1]
    down = half_specs(shared)[2]
    wide = pl.BlockSpec((block, hidden), lambda i: (i, 0))
    return pl.pallas_call(
        dz_kernel,
        out_shape=(
            jax.ShapeDtypeStruct((count, hidden), BF),
            jax.ShapeDtypeStruct((1, hidden), F32),
        ),
        grid=(count // block,),
        in_specs=[pl.BlockSpec((block, width), lambda i: (i, 0)), down, wide],
        out_specs=(wide, pl.BlockSpec((1, hidden), lambda i: (0, 0))),
        cost_estimate=pl.CostEstimate(
            flops=2 * count * width * hidden,
            bytes_accessed=2 * (count * width + 2 * count * hidden + width * hidden),
            transcendentals=0,
        ),
        compiler_params=pltpu.CompilerParams(vmem_limit_bytes=60 << 20),
    )(dy, shared, slope)


def g_one_kernel(d_ref, w_ref, normed_ref, gain_ref, h_ref, sums_ref, bias_ref):
    @pl.when(pl.program_id(0) == 0)
    def _():
        sums_ref[...] = jnp.zeros_like(sums_ref)
        bias_ref[...] = jnp.zeros_like(bias_ref)

    d = d_ref[...]
    bias_ref[...] += jnp.sum(d.astype(F32), 0, keepdims=True)
    width = h_ref.shape[1]
    chunk = math.gcd(width, 512)
    for start in range(0, width, chunk):
        here = slice(start, start + chunk)
        g = dot_nt(d, w_ref[here, :])
        h_ref[:, here] = (g * gain_ref[:, here]).astype(BF)
        sums_ref[0:1, here] += jnp.sum(g * normed_ref[:, here].astype(F32), 0, keepdims=True)
        sums_ref[1:2, here] += jnp.sum(g, 0, keepdims=True)


def pull_one(d, weights, normed, gain, block):
    count, inner = d.shape
    width = gain.shape[1]
    return pl.pallas_call(
        g_one_kernel,
        out_shape=(
            jax.ShapeDtypeStruct((count, width), BF),
            jax.ShapeDtypeStruct((2, width), F32),
            jax.ShapeDtypeStruct((1, inner), F32),
        ),
        grid=(count // block,),
        in_specs=[
            pl.BlockSpec((block, inner), lambda i: (i, 0)),
            pl.BlockSpec((width, inner), lambda i: (0, 0)),
            pl.BlockSpec((block, width), lambda i: (i, 0)),
            pl.BlockSpec((1, width), lambda i: (0, 0)),
        ],
        out_specs=(
            pl.BlockSpec((block, width), lambda i: (i, 0)),
            pl.BlockSpec((2, width), lambda i: (0, 0)),
            pl.BlockSpec((1, inner), lambda i: (0, 0)),
        ),
        cost_estimate=pl.CostEstimate(
            flops=2 * count * width * inner,
            bytes_accessed=2 * count * (inner + 2 * width),
            transcendentals=0,
        ),
        compiler_params=pltpu.CompilerParams(vmem_limit_bytes=60 << 20),
    )(d, weights, normed, gain)


def split_rows(core, value_ref, kept_ref, sent_ref, cols, extra):
    planes, _, rows, _ = kept_ref.shape
    for p in range(planes):
        own = pl.ds(pl.multiple_of((2 * p + core) * rows, rows), rows)
        other = pl.ds(pl.multiple_of((2 * p + 1 - core) * rows, rows), rows)
        kept = value_ref[own, :]
        kept_ref[p, 0, :, cols] = kept if extra is None else kept + extra(p)
        sent_ref[p, 0, :, cols] = value_ref[other, :].astype(BF)


def g_two_kernel(
    core_ref, d_ref, low_ref, high_ref, normed_ref, gain_ref, h_ref, kept_ref, sent_ref, sums_ref, value_s
):
    @pl.when((pl.program_id(0) == 0) & (pl.program_id(1) == 0))
    def _():
        sums_ref[...] = jnp.zeros_like(sums_ref)

    _, rows, width = low_ref.shape
    chunk = value_s.shape[1]
    for start in range(0, width, chunk):
        here = slice(start, start + chunk)
        part = slice(start // rows, (start + chunk) // rows)
        g = dot_nt(d_ref[:, :width], low_ref[part, :, :].reshape(chunk, width))
        g += dot_nt(d_ref[:, width:], high_ref[part, :, :].reshape(chunk, width))
        value_s[...] = g * gain_ref[:, here] + h_ref[:, here].astype(F32)
        sums_ref[0:1, here] += jnp.sum(g * normed_ref[:, here].astype(F32), 0, keepdims=True)
        sums_ref[1:2, here] += jnp.sum(g, 0, keepdims=True)
        split_rows(core_ref[0], value_s, kept_ref, sent_ref, here, None)


def token_specs(planes, per_chip, rows, width, group):
    full = planes // group
    piece = pl.BlockSpec((group, 1, rows, width), lambda s, p, core: (p, s, 0, 0))

    def block(cols):
        return pl.BlockSpec((2 * group * rows, cols), lambda s, p, core: (s * full + p, 0))

    return (per_chip, full), piece, block


def pull_two(core, d, shared, normed, gain, h_one, planes, per_chip, rows):
    count, inner = d.shape
    width = gain.shape[1]
    group = math.gcd(planes, 2)
    grid, piece, block = token_specs(planes, per_chip, rows, width, group)
    low, high, _ = half_specs(shared)
    shape = (planes, per_chip, rows, width)
    return pl.pallas_call(
        g_two_kernel,
        out_shape=(
            jax.ShapeDtypeStruct(shape, F32),
            jax.ShapeDtypeStruct(shape, BF),
            jax.ShapeDtypeStruct((2, width), F32),
        ),
        grid_spec=pltpu.PrefetchScalarGridSpec(
            num_scalar_prefetch=1,
            grid=grid,
            in_specs=[
                block(inner),
                low,
                high,
                block(width),
                pl.BlockSpec((1, width), lambda s, p, core: (0, 0)),
                block(width),
            ],
            out_specs=(piece, piece, pl.BlockSpec((2, width), lambda s, p, core: (0, 0))),
            scratch_shapes=[pltpu.VMEM((2 * group * rows, math.gcd(width, 512)), F32)],
        ),
        cost_estimate=pl.CostEstimate(
            flops=2 * count * width * inner,
            bytes_accessed=2 * count * (inner + 4 * width),
            transcendentals=0,
        ),
        compiler_params=pltpu.CompilerParams(vmem_limit_bytes=60 << 20),
    )(core.reshape(1), d, shared, shared, normed, gain, h_one)


def out_kernel(
    core_ref, z_ref, down_ref, ctx_ref, out_ref, x_ref, bias_ref, kept_ref, sent_ref, value_s
):
    chips, rows, width = down_ref.shape
    chunk = value_s.shape[1]
    for start in range(0, width, chunk):
        here = slice(start, start + chunk)
        value_s[...] = dot_nn(z_ref[...], down_ref[:, :, here].reshape(chips * rows, chunk)) + dot_nn(
            ctx_ref[...], out_ref[:, here]
        )
        split_rows(
            core_ref[0],
            value_s,
            kept_ref,
            sent_ref,
            here,
            lambda p: x_ref[p, 0, :, here].astype(F32) + bias_ref[:, here],
        )


def out_project(core, z, shared, context, w_out, x_mine, bias, planes, per_chip, rows):
    count, hidden = z.shape
    inner, width = w_out.shape
    group = math.gcd(planes, 2)
    grid, piece, block = token_specs(planes, per_chip, rows, width, group)
    down = half_specs(shared)[2]
    shape = (planes, per_chip, rows, width)
    return pl.pallas_call(
        out_kernel,
        out_shape=(jax.ShapeDtypeStruct(shape, F32), jax.ShapeDtypeStruct(shape, BF)),
        grid_spec=pltpu.PrefetchScalarGridSpec(
            num_scalar_prefetch=1,
            grid=grid,
            in_specs=[
                block(hidden),
                down,
                block(inner),
                pl.BlockSpec((inner, width), lambda s, p, core: (0, 0)),
                piece,
                pl.BlockSpec((1, width), lambda s, p, core: (0, 0)),
            ],
            out_specs=(piece, piece),
            scratch_shapes=[pltpu.VMEM((2 * group * rows, math.gcd(width, 512)), F32)],
        ),
        cost_estimate=pl.CostEstimate(
            flops=2 * count * width * (hidden + inner),
            bytes_accessed=2 * count * (hidden + inner + 4 * width),
            transcendentals=0,
        ),
        compiler_params=pltpu.CompilerParams(vmem_limit_bytes=60 << 20),
    )(core.reshape(1), z, shared, context, w_out, x_mine.reshape(shape), bias)


def ordered(value, *before):
    return lax.optimization_barrier((value,) + before)[0]


def local(
    tokens,
    ln1_gain,
    ln1_shift,
    ln2_gain,
    ln2_shift,
    qkv_weight,
    qkv_bias,
    out_weight,
    out_bias,
    in_weight,
    in_bias,
    down_weight,
    down_bias,
    cotangent,
):
    planes = lax.axis_size("pl")
    chips = lax.axis_size("dp") * planes
    n = 2 * chips
    flat = (lax.axis_index("dp") * planes + lax.axis_index("pl")) * 2 + lax.axis_index("core")
    core = lax.axis_index("core")
    first_core = core == 0
    seqs, rows_here, width = tokens.shape
    per_chip = seqs // planes
    length = rows_here * planes * 2
    count = per_chip * length
    heads = H // 2
    qkv_cols = heads * 3 * HD
    ctx_cols = heads * HD
    hidden = in_weight.shape[1] // 2
    own_rows = qkv_weight.shape[0]

    def swap(value, mask):
        return lax.ppermute(value, AXES, [(i, i ^ mask) for i in range(n)])

    def in_core_order(own, other, axis):
        return jnp.where(
            first_core, jnp.concatenate([own, other], axis), jnp.concatenate([other, own], axis)
        )

    def pick(value, index, axis):
        return lax.dynamic_index_in_dim(value, index, axis, keepdims=False)

    qkv_halves = (
        qkv_weight.reshape(own_rows, 2, heads // 2, 2, 3, HD)
        .transpose(1, 0, 2, 4, 3, 5)
        .reshape(2, own_rows, qkv_cols)
    )
    out_halves = out_weight.reshape(own_rows, 2, ctx_cols).transpose(1, 0, 2)
    in_halves = (
        in_weight.reshape(own_rows, chips, 2, hidden // chips)
        .transpose(2, 0, 1, 3)
        .reshape(2, own_rows, hidden)
    )
    halves = jnp.concatenate([qkv_halves, out_halves, in_halves], 2)
    chip_rows = in_core_order(pick(halves, core, 0), swap(pick(halves, 1 - core, 0), 1), 0)
    first_cols = qkv_cols + ctx_cols
    first_all = lax.all_gather(chip_rows[:, :first_cols], CHIPS, axis=0, tiled=True)
    small = jnp.concatenate(
        [ln1_gain, ln1_shift, ln2_gain, ln2_shift, out_bias, down_bias, qkv_bias, in_bias]
    )
    small = jnp.broadcast_to(small[None, :], (n, small.shape[0]))
    small = ordered(small, chip_rows)
    small = lax.all_to_all(small, AXES, split_axis=0, concat_axis=0, tiled=True)
    small = small.astype(F32)
    part = width // n
    gain_one, shift_one, gain_two, shift_two, b_out, b_down = (
        small[:, i * part : (i + 1) * part].reshape(width) for i in range(6)
    )
    b_qkv = small[:, 6 * part : 9 * part].reshape(2, heads // 2, 2, 3, HD)
    b_qkv = pick(b_qkv, core, 0).transpose(0, 2, 1, 3).reshape(qkv_cols)
    b_in = pick(small[:, 9 * part :].reshape(chips, 2, hidden // chips), core, 1).reshape(hidden)

    second = jnp.concatenate(
        [
            chip_rows[:, first_cols : first_cols + width],
            chip_rows[:, first_cols + width :],
            down_weight,
        ],
        0,
    )
    shared = lax.all_gather(second[None], CHIPS, axis=0, tiled=True)
    other_rows = lax.dynamic_slice(first_all, ((1 - core) * ctx_cols, qkv_cols), (ctx_cols, ctx_cols))
    some_rows = lax.dynamic_slice(first_all, (core * ctx_cols, qkv_cols), (ctx_cols, ctx_cols))
    w_out = in_core_order(some_rows, swap(other_rows, 1), 1)
    w_qkv = first_all[:, :qkv_cols]

    def to_chip(value):
        mine = lax.all_to_all(value, "pl", split_axis=0, concat_axis=0, tiled=True)
        return mine, swap(mine, 1)

    def to_tokens(kept, sent):
        value = (kept + swap(sent, 1).astype(F32)).astype(BF)
        value = value.reshape(seqs, rows_here, width)
        return lax.all_to_all(value, "pl", split_axis=0, concat_axis=0, tiled=True)

    x_mine, x_theirs = to_chip(ordered(tokens, chip_rows))
    dy_mine, dy_theirs = to_chip(ordered(cotangent, x_mine))
    gains = jnp.stack([gain_one, shift_one, gain_two, shift_two])
    dy = arrange_cotangent(core, dy_mine, dy_theirs, per_chip)
    a_one, a_two, normed = normalize(core, x_mine, x_theirs, gains, per_chip)

    qkv = (dot_nn(a_one, w_qkv) + b_qkv).astype(BF)
    context_grad = dot_nt(dy, w_out).astype(BF)
    context, qkv_grad = attention(
        qkv.reshape(per_chip, length, qkv_cols),
        context_grad.reshape(per_chip, length, ctx_cols),
        rotary_lanes(length),
    )
    context = context.reshape(count, ctx_cols)
    qkv_grad = qkv_grad.reshape(count, qkv_cols)

    chip_bits = chips.bit_length() - 1
    plane_bits = planes.bit_length() - 1

    def scatter_sum(value, order):
        cols = value.shape[1]
        value = value.reshape((2,) * chip_bits + (value.shape[0] // chips, cols))
        left = list(range(chip_bits, 0, -1))
        for step, bit in enumerate(order):
            axis = left.index(bit)
            left.remove(bit)
            mine = (flat >> bit) & 1
            sent = swap(pick(value, 1 - mine, axis).astype(BF), 1 << bit)
            value = pick(value, mine, axis).astype(F32) + sent.astype(F32)
            if step < len(order) - 1:
                value = value.astype(BF)
        return value

    plane_up = list(range(1, plane_bits + 1))
    plane_down = plane_up[::-1]
    beyond = list(range(plane_bits + 1, chip_bits + 1))
    orders = {
        "sda": plane_up + beyond,
        "sdb": beyond + plane_down,
        "sia": plane_down + beyond,
        "sib": beyond + plane_up,
    }

    def scatter_two_ways(value, tag):
        cols = value.shape[1] // 2
        return jnp.concatenate(
            [
                scatter_sum(value[:, :cols], orders[tag + "a"]),
                scatter_sum(value[:, cols:], orders[tag + "b"]),
            ],
            1,
        )

    def own_rows_of(value):
        value = value.reshape(2, own_rows, value.shape[1])
        return in_core_order(
            pick(value, core, 0)[:, None], swap(pick(value, 1 - core, 0), 1)[:, None], 1
        )

    out_w_grad = dot_tn(context, dy).astype(BF)
    other_cols = lax.dynamic_slice_in_dim(out_w_grad, (1 - core) * ctx_cols, ctx_cols, 1)
    own_cols = lax.dynamic_slice_in_dim(out_w_grad, core * ctx_cols, ctx_cols, 1)
    out_w_grad = in_core_order(own_cols, swap(other_cols, 1), 0)
    qkv_w_grad = dot_tn(a_one, qkv_grad).astype(BF)
    first_grad = jnp.concatenate([qkv_w_grad, out_w_grad], 1)
    first_grad = lax.psum_scatter(first_grad, CHIPS, scatter_dimension=0, tiled=True)
    first_grad = own_rows_of(first_grad.astype(F32))
    qkv_w_grad = (
        first_grad[:, :, :qkv_cols]
        .reshape(own_rows, 2, heads // 2, 3, 2, HD)
        .transpose(0, 1, 2, 4, 3, 5)
        .reshape(own_rows, 2 * qkv_cols)
    )
    out_w_grad = first_grad[:, :, qkv_cols:].reshape(own_rows, width)
    block = math.gcd(count, 512)
    h_one, sums_one, qkv_b_grad = pull_one(qkv_grad, first_all, normed, gain_one[None], block)

    z, slope = up_project(a_two, shared, b_in[None], block)
    down_w_grad = dot_tn(z, dy).astype(BF)
    down_w_grad = scatter_two_ways(down_w_grad, "sd")
    du, in_b_grad = down_pull(dy, shared, slope, block)
    in_w_grad = dot_tn(a_two, du).astype(BF)
    in_w_grad = own_rows_of(scatter_two_ways(in_w_grad, "si"))
    in_w_grad = (
        in_w_grad.reshape(own_rows, 2, chips, hidden // chips)
        .transpose(0, 2, 1, 3)
        .reshape(own_rows, 2 * hidden)
    )
    kept, sent, sums_two = pull_two(
        core, du, shared, normed, gain_two[None], h_one, planes, per_chip, rows_here
    )
    combined = to_tokens(kept, sent)
    kept, sent = out_project(
        core, z, shared, context, w_out, x_mine, (b_out + b_down)[None], planes, per_chip, rows_here
    )
    output = to_tokens(kept, sent)

    x_here = tokens.astype(F32)
    mean_here = jnp.mean(x_here, axis=-1, keepdims=True)
    centred_here = x_here - mean_here
    scale_here = lax.rsqrt(jnp.mean(centred_here * centred_here, axis=-1, keepdims=True) + epsilon)
    normed_here = centred_here * scale_here
    combined = combined.astype(F32)
    pulled = (
        combined
        - jnp.mean(combined, axis=-1, keepdims=True)
        - normed_here * jnp.mean(combined * normed_here, axis=-1, keepdims=True)
    ) * scale_here
    dy_here = cotangent.astype(F32)
    input_grad = dy_here + pulled

    qkv_b_grad = (
        qkv_b_grad.reshape(heads // 2, 3, 2, HD)
        .transpose(0, 2, 1, 3)
        .reshape(qkv_cols)
    )
    nothing = jnp.zeros_like(qkv_b_grad)
    qkv_b_grad = in_core_order(qkv_b_grad, nothing, 0)
    in_b_grad = in_b_grad.reshape(chips, hidden // chips)
    in_b_grad = in_core_order(in_b_grad[:, None], jnp.zeros_like(in_b_grad)[:, None], 1)
    sums = [
        sums_one[0],
        sums_one[1],
        sums_two[0],
        sums_two[1],
        jnp.sum(dy_here, (0, 1)),
        qkv_b_grad,
        in_b_grad,
    ]
    sums = jnp.concatenate([value.reshape(n, -1) for value in sums], 1)
    sums = lax.all_to_all(sums, AXES, split_axis=0, concat_axis=0, tiled=True)
    sums = jnp.sum(sums, 0)
    b_grad = sums[4 * part : 5 * part]
    return (
        output,
        input_grad,
        sums[:part],
        sums[part : 2 * part],
        sums[2 * part : 3 * part],
        sums[3 * part : 4 * part],
        qkv_w_grad,
        sums[5 * part : 8 * part],
        out_w_grad,
        b_grad,
        in_w_grad,
        sums[8 * part :],
        down_w_grad,
        b_grad,
    )


def solution(mesh):
    split = Mesh(
        mesh.devices.reshape(mesh.shape["dp"], mesh.shape["seq"] // 2, 2),
        AXES,
    )
    rows = P("dp", ("pl", "core"), None)
    vector = P(AXES)
    matrix = P(AXES, None)
    return jax.shard_map(
        local,
        mesh=split,
        in_specs=(
            rows,
            vector,
            vector,
            vector,
            vector,
            matrix,
            vector,
            matrix,
            vector,
            matrix,
            vector,
            matrix,
            vector,
            rows,
        ),
        out_specs=(
            rows,
            rows,
            vector,
            vector,
            vector,
            vector,
            matrix,
            vector,
            matrix,
            vector,
            matrix,
            vector,
            matrix,
            vector,
        ),
        check_vma=False,
    )
```

```python
import functools
import math

import jax
import jax.numpy as jnp
from jax import lax
from jax.experimental import pallas as pl
from jax.experimental.pallas import tpu as pltpu
from jax.sharding import Mesh
from jax.sharding import PartitionSpec as P


H = 16
HD = 64
ROT = 16
PAIR = 2 * HD
AXES = ("dp", "pl", "core")
CHIPS = ("dp", "pl")
BF = jnp.bfloat16
F32 = jnp.float32

epsilon = 1e-05


def dot_nn(left, right):
    return lax.dot_general(left, right, (((1,), (0,)), ((), ())), preferred_element_type=F32)


def dot_nt(left, right):
    return lax.dot_general(left, right, (((1,), (1,)), ((), ())), preferred_element_type=F32)


def dot_tn(left, right):
    return lax.dot_general(left, right, (((0,), (0,)), ((), ())), preferred_element_type=F32)


def rotary_lanes(length):
    lane = jnp.arange(PAIR, dtype=jnp.int32) % HD
    half = ROT // 2
    inverse = jnp.exp((lane % half).astype(F32) * (-2.0 * math.log(10000.0) / ROT))
    angles = jnp.arange(length, dtype=F32)[:, None] * inverse[None, :]
    turned = (lane < ROT)[None, :]
    first = (lane < half)[None, :]
    sines = jnp.sin(angles)
    return (
        jnp.where(turned, jnp.cos(angles), 1.0),
        jnp.where(first, -sines, 0.0),
        jnp.where(turned & ~first, sines, 0.0),
    )


def attention_kernel(
    block,
    qkv_ref,
    dc_ref,
    cos_ref,
    sin_a_ref,
    sin_b_ref,
    ctx_ref,
    dqkv_ref,
    q_s,
    k_s,
    kt_s,
    vt_s,
    ctxt_s,
    dqt_s,
    dk_s,
    dv_s,
):
    length = qkv_ref.shape[1]
    half = ROT // 2
    factor = 1.0 / math.sqrt(HD)
    value_cols = slice(2 * PAIR, 3 * PAIR)

    def turn(z, sign):
        swapped = pltpu.roll(z, PAIR - half, 1) * sin_a_ref[...] + pltpu.roll(z, half, 1) * sin_b_ref[...]
        return z * cos_ref[...] + sign * swapped

    q_s[...] = turn(qkv_ref[0, :, 0:PAIR].astype(F32), 1.0).astype(BF) * BF(factor)
    keys = turn(qkv_ref[0, :, PAIR : 2 * PAIR].astype(F32), 1.0).astype(BF)
    k_s[...] = keys
    kt_s[...] = keys.T
    vt_s[...] = qkv_ref[0, :, value_cols].T
    dk_s[...] = jnp.zeros_like(dk_s)
    dv_s[...] = jnp.zeros_like(dv_s)
    lane = lax.broadcasted_iota(jnp.int32, (1, PAIR), 1)
    keys_at = lax.broadcasted_iota(jnp.int32, (block, block), 0)
    queries_at = lax.broadcasted_iota(jnp.int32, (block, block), 1)
    chosen = [((lane >= h * HD) & (lane < h * HD + HD)).astype(BF) for h in range(2)]

    def front(h, i):
        lo, hi = i * block, (i + 1) * block
        queries = q_s[lo:hi, :] * chosen[h]
        grads = dc_ref[0, lo:hi, :] * chosen[h]
        scores = dot_nt(k_s[0:hi, :], queries)
        return scores, dot_nt(qkv_ref[0, 0:hi, value_cols], grads), queries, grads

    def middle(i, scores, weight_grad, queries, grads):
        lo, hi = i * block, (i + 1) * block
        last = jnp.where(keys_at <= queries_at, scores[lo:hi, :], -1e30)
        scores = jnp.concatenate([scores[:lo, :], last], 0) if i else last
        weights = jnp.exp(scores - jnp.max(scores, axis=0, keepdims=True))
        weights = weights * (1.0 / jnp.sum(weights, axis=0, keepdims=True))
        mixed = jnp.sum(weights * weight_grad, axis=0, keepdims=True)
        score_grad = (weights * (weight_grad - mixed)).astype(BF)
        return weights.astype(BF), score_grad, queries, grads

    def back(h, i, weights, score_grad, queries, grads):
        lo, hi = i * block, (i + 1) * block
        dims = slice(h * HD, h * HD + HD)
        ctxt_s[dims, lo:hi] = dot_nn(vt_s[dims, 0:hi], weights)
        dv_s[0:hi, :] += dot_nn(weights, grads)
        dk_s[0:hi, :] += dot_nn(score_grad, queries)
        dqt_s[dims, lo:hi] = dot_nn(kt_s[dims, 0:hi], score_grad)

    order = [(h, i) for i in range(length // block) for h in range(2)]
    ahead = front(*order[0])
    behind = None
    for step, (h, i) in enumerate(order):
        following = front(*order[step + 1]) if step + 1 < len(order) else None
        results = middle(i, *ahead)
        if behind is not None:
            back(*behind)
        behind = (h, i, *results)
        ahead = following
    back(*behind)
    ctx_ref[0] = ctxt_s[...].T.astype(BF)
    dqkv_ref[0, :, 0:PAIR] = turn(dqt_s[...].T * factor, -1.0).astype(BF)
    dqkv_ref[0, :, PAIR : 2 * PAIR] = turn(dk_s[...], -1.0).astype(BF)
    dqkv_ref[0, :, value_cols] = dv_s[...].astype(BF)


def attention(qkv, context_grad, tables):
    seqs, length, width = qkv.shape
    pairs = width // (3 * PAIR)
    table = pl.BlockSpec((length, PAIR), lambda s, h: (0, 0))
    wide = pl.BlockSpec((1, length, 3 * PAIR), lambda s, h: (s, 0, h))
    slim = pl.BlockSpec((1, length, PAIR), lambda s, h: (s, 0, h))
    return pl.pallas_call(
        functools.partial(attention_kernel, math.gcd(length, 256)),
        out_shape=(
            jax.ShapeDtypeStruct((seqs, length, width // 3), BF),
            jax.ShapeDtypeStruct((seqs, length, width), BF),
        ),
        grid=(seqs, pairs),
        in_specs=[wide, slim, table, table, table],
        out_specs=(slim, wide),
        scratch_shapes=[pltpu.VMEM((length, PAIR), BF)] * 2
        + [pltpu.VMEM((PAIR, length), BF)] * 2
        + [pltpu.VMEM((PAIR, length), F32)] * 2
        + [pltpu.VMEM((length, PAIR), F32)] * 2,
        cost_estimate=pl.CostEstimate(
            flops=seqs * pairs * 2 * 7 * length * length * PAIR,
            bytes_accessed=seqs * length * width * 6,
            transcendentals=seqs * pairs * length * length,
        ),
        compiler_params=pltpu.CompilerParams(vmem_limit_bytes=60 << 20),
    )(qkv, context_grad, *tables)


def both_cores(core, rows, mine_ref, theirs_ref):
    yield pl.ds(pl.multiple_of(core * rows, rows), rows), mine_ref[0]
    yield pl.ds(pl.multiple_of((1 - core) * rows, rows), rows), theirs_ref[0]


def norm_kernel(core_ref, mine_ref, theirs_ref, gains_ref, one_ref, two_ref, normed_ref):
    for at, value in both_cores(core_ref[0], mine_ref.shape[1], mine_ref, theirs_ref):
        x = value.astype(F32)
        centred = x - jnp.mean(x, axis=-1, keepdims=True)
        normed = centred * lax.rsqrt(jnp.mean(centred * centred, axis=-1, keepdims=True) + epsilon)
        one_ref[at, :] = (normed * gains_ref[0:1, :] + gains_ref[1:2, :]).astype(BF)
        two_ref[at, :] = (normed * gains_ref[2:3, :] + gains_ref[3:4, :]).astype(BF)
        normed_ref[at, :] = normed.astype(BF)


def dy_kernel(core_ref, mine_ref, theirs_ref, dy_ref, sum_ref):
    @pl.when((pl.program_id(0) == 0) & (pl.program_id(1) == 0))
    def _():
        sum_ref[...] = jnp.zeros_like(sum_ref)

    sum_ref[...] += jnp.sum(mine_ref[0].astype(F32), 0, keepdims=True)
    for at, value in both_cores(core_ref[0], mine_ref.shape[1], mine_ref, theirs_ref):
        dy_ref[at, :] = value


def on_pairs(kernel, outputs, core, mine, theirs, per_chip, extra=(), sums=0):
    blocks, rows, width = mine.shape
    planes = blocks // per_chip
    source = pl.BlockSpec((1, rows, width), lambda s, p, core: (p * per_chip + s, 0, 0))
    target = pl.BlockSpec((2 * rows, width), lambda s, p, core: (s * planes + p, 0))
    shape = jax.ShapeDtypeStruct((2 * blocks * rows, width), BF)
    whole = [pl.BlockSpec(value.shape, lambda s, p, core: (0, 0)) for value in extra]
    return pl.pallas_call(
        kernel,
        out_shape=(shape,) * outputs + (jax.ShapeDtypeStruct((1, width), F32),) * sums,
        grid_spec=pltpu.PrefetchScalarGridSpec(
            num_scalar_prefetch=1,
            grid=(per_chip, planes),
            in_specs=[source, source] + whole,
            out_specs=(target,) * outputs
            + (pl.BlockSpec((1, width), lambda s, p, core: (0, 0)),) * sums,
        ),
        cost_estimate=pl.CostEstimate(
            flops=20 * blocks * rows * width,
            bytes_accessed=(4 + 4 * outputs) * blocks * rows * width,
            transcendentals=0,
        ),
    )(core.reshape(1), mine, theirs, *extra)


def weave(first_core, own, other, chips):
    rows, hidden = own.shape
    block = hidden // chips

    def kernel(first_ref, own_ref, other_ref, out_ref):
        first = first_ref[0] == 1
        for chip in range(chips):
            here = slice(chip * block, (chip + 1) * block)
            mine, theirs = own_ref[:, here], other_ref[:, here]
            at = 2 * chip * block
            out_ref[:, at : at + block] = jnp.where(first, mine, theirs)
            out_ref[:, at + block : at + 2 * block] = jnp.where(first, theirs, mine)

    whole = pl.BlockSpec(memory_space=pltpu.VMEM)
    return pl.pallas_call(
        kernel,
        out_shape=jax.ShapeDtypeStruct((rows, 2 * hidden), own.dtype),
        in_specs=[pl.BlockSpec(memory_space=pltpu.SMEM), whole, whole],
        out_specs=whole,
    )(first_core.astype(jnp.int32).reshape(1), own, other)


def phi(u):
    density = jnp.exp(-0.5 * u * u) * (1.0 / math.sqrt(2.0 * math.pi))
    return 0.5 * (1.0 + lax.erf(u * math.sqrt(0.5))), density


def pipelined(chunks, first, second):
    ahead = first(chunks[0])
    for n, chunk in enumerate(chunks):
        following = first(chunks[n + 1]) if n + 1 < len(chunks) else None
        second(chunk, ahead)
        ahead = following


def starts(width, chunk=512):
    chunk = math.gcd(width, chunk)
    return [slice(at, at + chunk) for at in range(0, width, chunk)]


def stacked(ref, rows, cols):
    size = ref.shape[1]
    part = ref[rows.start // size : rows.stop // size, :, cols]
    return part.reshape(part.shape[0] * size, part.shape[2])


def shared_specs(shared):
    chips, rows, width = shared.shape
    low = pl.BlockSpec((chips, rows // 4, width), lambda *i: (0, 0, 0))
    high = pl.BlockSpec((chips, rows // 4, width), lambda *i: (0, 1, 0))
    down = pl.BlockSpec((chips, rows // 2, width), lambda *i: (0, 1, 0))
    return low, high, down


def up_kernel(a_ref, low_ref, high_ref, bias_ref, z_ref, slope_ref):
    width = low_ref.shape[2]
    everything = slice(0, a_ref.shape[1])
    a = a_ref[...]
    chunks = [
        (w_ref, here, slice(half * width + here.start, half * width + here.stop))
        for half, w_ref in enumerate((low_ref, high_ref))
        for here in starts(width, 256)
    ]

    def product(chunk):
        w_ref, here, there = chunk
        return dot_nn(a, stacked(w_ref, everything, here)) + bias_ref[:, there]

    def activate(chunk, u):
        there = chunk[2]
        cdf, density = phi(u)
        z_ref[:, there] = (u * cdf).astype(BF)
        slope_ref[:, there] = (cdf + u * density).astype(BF)

    pipelined(chunks, product, activate)


def up_project(a, shared, bias, block):
    count, width = a.shape
    hidden = bias.shape[1]
    low, high, _ = shared_specs(shared)
    wide = pl.BlockSpec((block, hidden), lambda i: (i, 0))
    shape = jax.ShapeDtypeStruct((count, hidden), BF)
    return pl.pallas_call(
        up_kernel,
        out_shape=(shape, shape),
        grid=(count // block,),
        in_specs=[
            pl.BlockSpec((block, width), lambda i: (i, 0)),
            low,
            high,
            pl.BlockSpec((1, hidden), lambda i: (0, 0)),
        ],
        out_specs=(wide, wide),
        cost_estimate=pl.CostEstimate(
            flops=2 * count * width * hidden,
            bytes_accessed=2 * (count * width + 2 * count * hidden + width * hidden),
            transcendentals=2 * count * hidden,
        ),
        compiler_params=pltpu.CompilerParams(vmem_limit_bytes=60 << 20),
    )(a, shared, shared, bias)


def dz_kernel(dy_ref, down_ref, slope_ref, du_ref, sum_ref):
    dy = dy_ref[...]
    everything = slice(0, dy.shape[1])

    @pl.when(pl.program_id(0) == 0)
    def _():
        sum_ref[...] = jnp.zeros_like(sum_ref)

    def product(here):
        return dot_nt(dy, stacked(down_ref, here, everything))

    def scale(here, dz):
        du = (dz * slope_ref[:, here].astype(F32)).astype(BF)
        du_ref[:, here] = du
        sum_ref[:, here] += jnp.sum(du.astype(F32), 0, keepdims=True)

    pipelined(starts(du_ref.shape[1]), product, scale)


def down_pull(dy, shared, slope, block):
    count, width = dy.shape
    hidden = slope.shape[1]
    wide = pl.BlockSpec((block, hidden), lambda i: (i, 0))
    return pl.pallas_call(
        dz_kernel,
        out_shape=(
            jax.ShapeDtypeStruct((count, hidden), BF),
            jax.ShapeDtypeStruct((1, hidden), F32),
        ),
        grid=(count // block,),
        in_specs=[
            pl.BlockSpec((block, width), lambda i: (i, 0)),
            shared_specs(shared)[2],
            wide,
        ],
        out_specs=(wide, pl.BlockSpec((1, hidden), lambda i: (0, 0))),
        cost_estimate=pl.CostEstimate(
            flops=2 * count * width * hidden,
            bytes_accessed=2 * (count * width + 2 * count * hidden + width * hidden),
            transcendentals=0,
        ),
        compiler_params=pltpu.CompilerParams(vmem_limit_bytes=60 << 20),
    )(dy, shared, slope)


def g_one_kernel(d_ref, w_ref, normed_ref, gain_ref, h_ref, sums_ref, bias_ref):
    @pl.when(pl.program_id(0) == 0)
    def _():
        sums_ref[...] = jnp.zeros_like(sums_ref)
        bias_ref[...] = jnp.zeros_like(bias_ref)

    d = d_ref[...]

    def product(here):
        return dot_nt(d, w_ref[here, :])

    def scale(here, g):
        h_ref[:, here] = (g * gain_ref[:, here]).astype(BF)
        sums_ref[0:1, here] += jnp.sum(g * normed_ref[:, here].astype(F32), 0, keepdims=True)
        sums_ref[1:2, here] += jnp.sum(g, 0, keepdims=True)

    pipelined(starts(h_ref.shape[1]), product, scale)
    bias_ref[...] += jnp.sum(d.astype(F32), 0, keepdims=True)


def pull_one(d, weights, normed, gain, block):
    count, inner = d.shape
    width = gain.shape[1]
    return pl.pallas_call(
        g_one_kernel,
        out_shape=(
            jax.ShapeDtypeStruct((count, width), BF),
            jax.ShapeDtypeStruct((2, width), F32),
            jax.ShapeDtypeStruct((1, inner), F32),
        ),
        grid=(count // block,),
        in_specs=[
            pl.BlockSpec((block, inner), lambda i: (i, 0)),
            pl.BlockSpec((width, inner), lambda i: (0, 0)),
            pl.BlockSpec((block, width), lambda i: (i, 0)),
            pl.BlockSpec((1, width), lambda i: (0, 0)),
        ],
        out_specs=(
            pl.BlockSpec((block, width), lambda i: (i, 0)),
            pl.BlockSpec((2, width), lambda i: (0, 0)),
            pl.BlockSpec((1, inner), lambda i: (0, 0)),
        ),
        cost_estimate=pl.CostEstimate(
            flops=2 * count * width * inner,
            bytes_accessed=2 * count * (inner + 2 * width),
            transcendentals=0,
        ),
        compiler_params=pltpu.CompilerParams(vmem_limit_bytes=60 << 20),
    )(d, weights, normed, gain)


def split_rows(core, value_ref, kept_ref, sent_ref, cols, extra):
    planes, _, rows, _ = kept_ref.shape
    for p in range(planes):
        own = pl.ds(pl.multiple_of((2 * p + core) * rows, rows), rows)
        other = pl.ds(pl.multiple_of((2 * p + 1 - core) * rows, rows), rows)
        kept = value_ref[own, :]
        kept_ref[p, 0, :, cols] = kept if extra is None else kept + extra(p)
        sent_ref[p, 0, :, cols] = value_ref[other, :].astype(BF)


def g_two_kernel(
    core_ref,
    d_ref,
    low_ref,
    high_ref,
    normed_ref,
    gain_ref,
    h_ref,
    kept_ref,
    sent_ref,
    sums_ref,
    value_s,
):
    @pl.when((pl.program_id(0) == 0) & (pl.program_id(1) == 0))
    def _():
        sums_ref[...] = jnp.zeros_like(sums_ref)

    width = low_ref.shape[2]
    everything = slice(0, width)

    def product(here):
        return dot_nt(d_ref[:, :width], stacked(low_ref, here, everything)) + dot_nt(
            d_ref[:, width:], stacked(high_ref, here, everything)
        )

    def scale(here, g):
        value_s[...] = g * gain_ref[:, here] + h_ref[:, here].astype(F32)
        sums_ref[0:1, here] += jnp.sum(g * normed_ref[:, here].astype(F32), 0, keepdims=True)
        sums_ref[1:2, here] += jnp.sum(g, 0, keepdims=True)
        split_rows(core_ref[0], value_s, kept_ref, sent_ref, here, None)

    pipelined(starts(width), product, scale)


def token_specs(planes, per_chip, rows, width, group):
    full = planes // group
    piece = pl.BlockSpec((group, 1, rows, width), lambda s, p, core: (p, s, 0, 0))

    def block(cols):
        return pl.BlockSpec((2 * group * rows, cols), lambda s, p, core: (s * full + p, 0))

    return (per_chip, full), piece, block


def pull_two(core, d, shared, normed, gain, h_one, planes, per_chip, rows):
    count, inner = d.shape
    width = gain.shape[1]
    group = math.gcd(planes, 2)
    grid, piece, block = token_specs(planes, per_chip, rows, width, group)
    low, high, _ = shared_specs(shared)
    shape = (planes, per_chip, rows, width)
    return pl.pallas_call(
        g_two_kernel,
        out_shape=(
            jax.ShapeDtypeStruct(shape, F32),
            jax.ShapeDtypeStruct(shape, BF),
            jax.ShapeDtypeStruct((2, width), F32),
        ),
        grid_spec=pltpu.PrefetchScalarGridSpec(
            num_scalar_prefetch=1,
            grid=grid,
            in_specs=[
                block(inner),
                low,
                high,
                block(width),
                pl.BlockSpec((1, width), lambda s, p, core: (0, 0)),
                block(width),
            ],
            out_specs=(piece, piece, pl.BlockSpec((2, width), lambda s, p, core: (0, 0))),
            scratch_shapes=[pltpu.VMEM((2 * group * rows, math.gcd(width, 512)), F32)],
        ),
        cost_estimate=pl.CostEstimate(
            flops=2 * count * width * inner,
            bytes_accessed=2 * count * (inner + 4 * width),
            transcendentals=0,
        ),
        compiler_params=pltpu.CompilerParams(vmem_limit_bytes=60 << 20),
    )(core.reshape(1), d, shared, shared, normed, gain, h_one)


def out_kernel(
    core_ref, z_ref, down_ref, ctx_ref, out_ref, x_ref, bias_ref, kept_ref, sent_ref, value_s
):
    def product(here):
        down = stacked(down_ref, slice(0, z_ref.shape[1]), here)
        return dot_nn(z_ref[...], down) + dot_nn(ctx_ref[...], out_ref[:, here])

    def split(here, value):
        value_s[...] = value
        split_rows(
            core_ref[0],
            value_s,
            kept_ref,
            sent_ref,
            here,
            lambda p: x_ref[p, 0, :, here].astype(F32) + bias_ref[:, here],
        )

    pipelined(starts(out_ref.shape[1]), product, split)


def out_project(core, z, shared, context, w_out, x_mine, bias, planes, per_chip, rows):
    count, hidden = z.shape
    inner, width = w_out.shape
    group = math.gcd(planes, 2)
    grid, piece, block = token_specs(planes, per_chip, rows, width, group)
    shape = (planes, per_chip, rows, width)
    return pl.pallas_call(
        out_kernel,
        out_shape=(jax.ShapeDtypeStruct(shape, F32), jax.ShapeDtypeStruct(shape, BF)),
        grid_spec=pltpu.PrefetchScalarGridSpec(
            num_scalar_prefetch=1,
            grid=grid,
            in_specs=[
                block(hidden),
                shared_specs(shared)[2],
                block(inner),
                pl.BlockSpec((inner, width), lambda s, p, core: (0, 0)),
                piece,
                pl.BlockSpec((1, width), lambda s, p, core: (0, 0)),
            ],
            out_specs=(piece, piece),
            scratch_shapes=[pltpu.VMEM((2 * group * rows, math.gcd(width, 512)), F32)],
        ),
        cost_estimate=pl.CostEstimate(
            flops=2 * count * width * (hidden + inner),
            bytes_accessed=2 * count * (hidden + inner + 4 * width),
            transcendentals=0,
        ),
        compiler_params=pltpu.CompilerParams(vmem_limit_bytes=60 << 20),
    )(core.reshape(1), z, shared, context, w_out, x_mine.reshape(shape), bias)


def ordered(value, *before):
    return lax.optimization_barrier((value,) + before)[0]


def local(
    tokens,
    ln1_gain,
    ln1_shift,
    ln2_gain,
    ln2_shift,
    qkv_weight,
    qkv_bias,
    out_weight,
    out_bias,
    in_weight,
    in_bias,
    down_weight,
    down_bias,
    cotangent,
):
    planes = lax.axis_size("pl")
    chips = lax.axis_size("dp") * planes
    n = 2 * chips
    core = lax.axis_index("core")
    first_core = core == 0
    seqs, rows_here, width = tokens.shape
    per_chip = seqs // planes
    length = rows_here * planes * 2
    count = per_chip * length
    heads = H // 2
    qkv_cols = heads * 3 * HD
    ctx_cols = heads * HD
    hidden = in_weight.shape[1] // 2
    own_rows = qkv_weight.shape[0]

    def swap(value, mask):
        return lax.ppermute(value, AXES, [(i, i ^ mask) for i in range(n)])

    def in_core_order(own, other, axis):
        return jnp.where(
            first_core, jnp.concatenate([own, other], axis), jnp.concatenate([other, own], axis)
        )

    def pick(value, index, axis):
        return lax.dynamic_index_in_dim(value, index, axis, keepdims=False)

    qkv_halves = (
        qkv_weight.reshape(own_rows, 2, heads // 2, 2, 3, HD)
        .transpose(1, 0, 2, 4, 3, 5)
        .reshape(2, own_rows, qkv_cols)
    )
    out_halves = out_weight.reshape(own_rows, 2, ctx_cols).transpose(1, 0, 2)
    in_halves = (
        in_weight.reshape(own_rows, chips, 2, hidden // chips)
        .transpose(2, 0, 1, 3)
        .reshape(2, own_rows, hidden)
    )
    halves = jnp.concatenate([qkv_halves, out_halves, in_halves], 2)
    chip_rows = in_core_order(pick(halves, core, 0), swap(pick(halves, 1 - core, 0), 1), 0)
    first_cols = qkv_cols + ctx_cols
    first_all = lax.all_gather(chip_rows[:, :first_cols], CHIPS, axis=0, tiled=True)
    small = jnp.concatenate(
        [ln1_gain, ln1_shift, ln2_gain, ln2_shift, out_bias, down_bias, qkv_bias, in_bias]
    )
    small = jnp.broadcast_to(small[None, :], (n, small.shape[0]))
    small = ordered(small, chip_rows)
    small = lax.all_to_all(small, AXES, split_axis=0, concat_axis=0, tiled=True)
    small = small.astype(F32)
    part = width // n
    gain_one, shift_one, gain_two, shift_two, b_out, b_down = (
        small[:, i * part : (i + 1) * part].reshape(width) for i in range(6)
    )
    b_qkv = small[:, 6 * part : 9 * part].reshape(2, heads // 2, 2, 3, HD)
    b_qkv = pick(b_qkv, core, 0).transpose(0, 2, 1, 3).reshape(qkv_cols)
    b_in = pick(small[:, 9 * part :].reshape(chips, 2, hidden // chips), core, 1).reshape(hidden)

    deep = chips // planes
    second = jnp.concatenate(
        [
            chip_rows[:, first_cols : first_cols + width],
            chip_rows[:, first_cols + width :],
            down_weight,
        ],
        0,
    )
    shared = lax.all_gather(second[None], CHIPS, axis=0, tiled=True)
    other_rows = lax.dynamic_slice(first_all, ((1 - core) * ctx_cols, qkv_cols), (ctx_cols, ctx_cols))
    some_rows = lax.dynamic_slice(first_all, (core * ctx_cols, qkv_cols), (ctx_cols, ctx_cols))
    w_out = in_core_order(some_rows, swap(other_rows, 1), 1)
    w_qkv = first_all[:, :qkv_cols]

    def to_chip(value):
        mine = lax.all_to_all(value, "pl", split_axis=0, concat_axis=0, tiled=True)
        return mine, swap(mine, 1)

    def to_tokens(kept, sent):
        value = (kept + swap(sent, 1).astype(F32)).astype(BF)
        value = value.reshape(seqs, rows_here, width)
        return lax.all_to_all(value, "pl", split_axis=0, concat_axis=0, tiled=True)

    x_mine, x_theirs = to_chip(ordered(tokens, chip_rows))
    dy_mine, dy_theirs = to_chip(ordered(cotangent, x_mine))
    gains = jnp.stack([gain_one, shift_one, gain_two, shift_two])
    dy, dy_sum = on_pairs(dy_kernel, 1, core, dy_mine, dy_theirs, per_chip, sums=1)
    a_one, a_two, normed = on_pairs(
        norm_kernel, 3, core, x_mine, x_theirs, per_chip, (gains,)
    )

    qkv = (dot_nn(a_one, w_qkv) + b_qkv).astype(BF)
    context_grad = dot_nt(dy, w_out).astype(BF)
    context, qkv_grad = attention(
        qkv.reshape(per_chip, length, qkv_cols),
        context_grad.reshape(per_chip, length, ctx_cols),
        rotary_lanes(length),
    )
    context = context.reshape(count, ctx_cols)
    qkv_grad = qkv_grad.reshape(count, qkv_cols)

    plane_here = lax.axis_index("pl")
    deep_here = lax.axis_index("dp")

    def direct_sum(value, axis, size, here, stride, final):
        total = pick(value, here, axis).astype(F32)
        for k in range(1, size):
            total += swap(pick(value, here ^ k, axis), k * stride).astype(F32)
        return total if final else total.astype(BF)

    def plane_then_deep(value):
        value = value.reshape(deep, planes, value.shape[0] // chips, value.shape[1])
        value = direct_sum(value, 1, planes, plane_here, 2, False)
        return direct_sum(value, 0, deep, deep_here, 2 * planes, True)

    def deep_then_plane(value):
        value = value.reshape(deep, planes, value.shape[0] // chips, value.shape[1])
        value = direct_sum(value, 0, deep, deep_here, 2 * planes, False)
        return direct_sum(value, 0, planes, plane_here, 2, True)

    def own_rows_of(value):
        value = value.reshape(2, own_rows, value.shape[1])
        return pick(value, core, 0), swap(pick(value, 1 - core, 0), 1)

    out_w_grad = dot_tn(context, dy).astype(BF)
    other_cols = lax.dynamic_slice_in_dim(out_w_grad, (1 - core) * ctx_cols, ctx_cols, 1)
    own_cols = lax.dynamic_slice_in_dim(out_w_grad, core * ctx_cols, ctx_cols, 1)
    out_w_grad = in_core_order(own_cols, swap(other_cols, 1), 0)
    qkv_w_grad = dot_tn(a_one, qkv_grad).astype(BF)
    first_grad = jnp.concatenate([qkv_w_grad, out_w_grad], 1)
    first_grad = first_grad.reshape(deep, planes, 2 * own_rows, first_cols).transpose(1, 0, 2, 3)
    first_grad = lax.all_to_all(first_grad, "pl", split_axis=0, concat_axis=0, tiled=True)
    first_grad = jnp.sum(first_grad.astype(F32), 0).astype(BF)
    first_grad = direct_sum(first_grad, 0, deep, deep_here, 2 * planes, True)
    first_own, first_other = own_rows_of(first_grad)
    first_grad = in_core_order(first_own[:, None], first_other[:, None], 1)
    qkv_w_grad = (
        first_grad[:, :, :qkv_cols]
        .reshape(own_rows, 2, heads // 2, 3, 2, HD)
        .transpose(0, 1, 2, 4, 3, 5)
        .reshape(own_rows, 2 * qkv_cols)
    )
    out_w_grad = first_grad[:, :, qkv_cols:].reshape(own_rows, width)
    block = math.gcd(count, 512)
    h_one, sums_one, qkv_b_grad = pull_one(qkv_grad, first_all, normed, gain_one[None], block)

    z, slope = up_project(a_two, shared, b_in[None], block)
    down_w_grad = dot_tn(z, dy).astype(BF)
    down_w_grad = plane_then_deep(down_w_grad)
    du, in_b_grad = down_pull(dy, shared, slope, block)
    in_w_grad = dot_tn(a_two, du).astype(BF)
    in_w_grad = jnp.concatenate(
        [
            plane_then_deep(in_w_grad[:, : hidden // 2]),
            deep_then_plane(in_w_grad[:, hidden // 2 :]),
        ],
        1,
    )
    in_w_own, in_w_other = own_rows_of(in_w_grad)
    in_w_grad = weave(first_core, in_w_own, in_w_other, chips)
    kept, sent, sums_two = pull_two(
        core, du, shared, normed, gain_two[None], h_one, planes, per_chip, rows_here
    )
    combined = to_tokens(kept, sent)
    kept, sent = out_project(
        core, z, shared, context, w_out, x_mine, (b_out + b_down)[None], planes, per_chip, rows_here
    )
    output = to_tokens(kept, sent)

    x_here = tokens.astype(F32)
    mean_here = jnp.mean(x_here, axis=-1, keepdims=True)
    centred_here = x_here - mean_here
    scale_here = lax.rsqrt(jnp.mean(centred_here * centred_here, axis=-1, keepdims=True) + epsilon)
    normed_here = centred_here * scale_here
    combined = combined.astype(F32)
    pulled = (
        combined
        - jnp.mean(combined, axis=-1, keepdims=True)
        - normed_here * jnp.mean(combined * normed_here, axis=-1, keepdims=True)
    ) * scale_here
    dy_here = cotangent.astype(F32)
    input_grad = dy_here + pulled

    qkv_b_grad = (
        qkv_b_grad.reshape(heads // 2, 3, 2, HD)
        .transpose(0, 2, 1, 3)
        .reshape(qkv_cols)
    )
    nothing = jnp.zeros_like(qkv_b_grad)
    qkv_b_grad = in_core_order(qkv_b_grad, nothing, 0)
    in_b_grad = in_b_grad.reshape(chips, hidden // chips)
    in_b_grad = in_core_order(in_b_grad[:, None], jnp.zeros_like(in_b_grad)[:, None], 1)
    sums = [
        sums_one[0],
        sums_one[1],
        sums_two[0],
        sums_two[1],
        dy_sum,
        qkv_b_grad,
        in_b_grad,
    ]
    sums = jnp.concatenate([value.reshape(n, -1) for value in sums], 1)
    sums = lax.all_to_all(sums, AXES, split_axis=0, concat_axis=0, tiled=True)
    sums = jnp.sum(sums, 0)
    b_grad = sums[4 * part : 5 * part]
    return (
        output,
        input_grad,
        sums[:part],
        sums[part : 2 * part],
        sums[2 * part : 3 * part],
        sums[3 * part : 4 * part],
        qkv_w_grad,
        sums[5 * part : 8 * part],
        out_w_grad,
        b_grad,
        in_w_grad,
        sums[8 * part :],
        down_w_grad,
        b_grad,
    )


def solution(mesh):
    split = Mesh(
        mesh.devices.reshape(mesh.shape["dp"], mesh.shape["seq"] // 2, 2),
        AXES,
    )
    rows = P("dp", ("pl", "core"), None)
    vector = P(AXES)
    matrix = P(AXES, None)
    return jax.shard_map(
        local,
        mesh=split,
        in_specs=(
            rows,
            vector,
            vector,
            vector,
            vector,
            matrix,
            vector,
            matrix,
            vector,
            matrix,
            vector,
            matrix,
            vector,
            rows,
        ),
        out_specs=(
            rows,
            rows,
            vector,
            vector,
            vector,
            vector,
            matrix,
            vector,
            matrix,
            vector,
            matrix,
            vector,
            matrix,
            vector,
        ),
        check_vma=False,
    )
```

```python
import functools
import math

import jax
import jax.numpy as jnp
from jax import lax
from jax.experimental import pallas as pl
from jax.experimental.pallas import tpu as pltpu
from jax.sharding import Mesh
from jax.sharding import PartitionSpec as P


H = 16
HD = 64
ROT = 16
PAIR = 2 * HD
AXES = ("dp", "pl", "core")
CHIPS = ("dp", "pl")
BF = jnp.bfloat16
F32 = jnp.float32

epsilon = 1e-05


def dot_nn(left, right):
    return lax.dot_general(left, right, (((1,), (0,)), ((), ())), preferred_element_type=F32)


def dot_nt(left, right):
    return lax.dot_general(left, right, (((1,), (1,)), ((), ())), preferred_element_type=F32)


def dot_tn(left, right):
    return lax.dot_general(left, right, (((0,), (0,)), ((), ())), preferred_element_type=F32)


def rotary_lanes(length):
    lane = jnp.arange(PAIR, dtype=jnp.int32) % HD
    half = ROT // 2
    inverse = jnp.exp((lane % half).astype(F32) * (-2.0 * math.log(10000.0) / ROT))
    angles = jnp.arange(length, dtype=F32)[:, None] * inverse[None, :]
    turned = (lane < ROT)[None, :]
    first = (lane < half)[None, :]
    sines = jnp.sin(angles)
    return (
        jnp.where(turned, jnp.cos(angles), 1.0),
        jnp.where(first, -sines, 0.0),
        jnp.where(turned & ~first, sines, 0.0),
    )


def attention_kernel(
    block,
    qkv_ref,
    dc_ref,
    cos_ref,
    sin_a_ref,
    sin_b_ref,
    ctx_ref,
    dqkv_ref,
    q_s,
    k_s,
    kt_s,
    vt_s,
    ctxt_s,
    dqt_s,
    dk_s,
    dv_s,
):
    length = qkv_ref.shape[1]
    half = ROT // 2
    factor = 1.0 / math.sqrt(HD)
    value_cols = slice(2 * PAIR, 3 * PAIR)

    def turn(z, sign):
        swapped = pltpu.roll(z, PAIR - half, 1) * sin_a_ref[...] + pltpu.roll(z, half, 1) * sin_b_ref[...]
        return z * cos_ref[...] + sign * swapped

    q_s[...] = turn(qkv_ref[0, :, 0:PAIR].astype(F32), 1.0).astype(BF) * BF(factor)
    keys = turn(qkv_ref[0, :, PAIR : 2 * PAIR].astype(F32), 1.0).astype(BF)
    k_s[...] = keys
    kt_s[...] = keys.T
    vt_s[...] = qkv_ref[0, :, value_cols].T
    dk_s[...] = jnp.zeros_like(dk_s)
    dv_s[...] = jnp.zeros_like(dv_s)
    lane = lax.broadcasted_iota(jnp.int32, (1, PAIR), 1)
    keys_at = lax.broadcasted_iota(jnp.int32, (block, block), 0)
    queries_at = lax.broadcasted_iota(jnp.int32, (block, block), 1)
    chosen = [((lane >= h * HD) & (lane < h * HD + HD)).astype(BF) for h in range(2)]

    def front(h, i):
        lo, hi = i * block, (i + 1) * block
        queries = q_s[lo:hi, :] * chosen[h]
        grads = dc_ref[0, lo:hi, :] * chosen[h]
        scores = dot_nt(k_s[0:hi, :], queries)
        return scores, dot_nt(qkv_ref[0, 0:hi, value_cols], grads), queries, grads

    def middle(i, scores, weight_grad, queries, grads):
        lo, hi = i * block, (i + 1) * block
        last = jnp.where(keys_at <= queries_at, scores[lo:hi, :], -1e30)
        scores = jnp.concatenate([scores[:lo, :], last], 0) if i else last
        weights = jnp.exp(scores - jnp.max(scores, axis=0, keepdims=True))
        weights = weights * (1.0 / jnp.sum(weights, axis=0, keepdims=True))
        mixed = jnp.sum(weights * weight_grad, axis=0, keepdims=True)
        score_grad = (weights * (weight_grad - mixed)).astype(BF)
        return weights.astype(BF), score_grad, queries, grads

    def back(h, i, weights, score_grad, queries, grads):
        lo, hi = i * block, (i + 1) * block
        dims = slice(h * HD, h * HD + HD)
        ctxt_s[dims, lo:hi] = dot_nn(vt_s[dims, 0:hi], weights)
        dv_s[0:hi, :] += dot_nn(weights, grads)
        dk_s[0:hi, :] += dot_nn(score_grad, queries)
        dqt_s[dims, lo:hi] = dot_nn(kt_s[dims, 0:hi], score_grad)

    order = [(h, i) for i in range(length // block) for h in range(2)]
    ahead = front(*order[0])
    behind = None
    for step, (h, i) in enumerate(order):
        following = front(*order[step + 1]) if step + 1 < len(order) else None
        results = middle(i, *ahead)
        if behind is not None:
            back(*behind)
        behind = (h, i, *results)
        ahead = following
    back(*behind)
    ctx_ref[0] = ctxt_s[...].T.astype(BF)
    dqkv_ref[0, :, 0:PAIR] = turn(dqt_s[...].T * factor, -1.0).astype(BF)
    dqkv_ref[0, :, PAIR : 2 * PAIR] = turn(dk_s[...], -1.0).astype(BF)
    dqkv_ref[0, :, value_cols] = dv_s[...].astype(BF)


def attention(qkv, context_grad, tables):
    seqs, length, width = qkv.shape
    pairs = width // (3 * PAIR)
    table = pl.BlockSpec((length, PAIR), lambda s, h: (0, 0))
    wide = pl.BlockSpec((1, length, 3 * PAIR), lambda s, h: (s, 0, h))
    slim = pl.BlockSpec((1, length, PAIR), lambda s, h: (s, 0, h))
    return pl.pallas_call(
        functools.partial(attention_kernel, math.gcd(length, 256)),
        out_shape=(
            jax.ShapeDtypeStruct((seqs, length, width // 3), BF),
            jax.ShapeDtypeStruct((seqs, length, width), BF),
        ),
        grid=(seqs, pairs),
        in_specs=[wide, slim, table, table, table],
        out_specs=(slim, wide),
        scratch_shapes=[pltpu.VMEM((length, PAIR), BF)] * 2
        + [pltpu.VMEM((PAIR, length), BF)] * 2
        + [pltpu.VMEM((PAIR, length), F32)] * 2
        + [pltpu.VMEM((length, PAIR), F32)] * 2,
        cost_estimate=pl.CostEstimate(
            flops=seqs * pairs * 2 * 7 * length * length * PAIR,
            bytes_accessed=seqs * length * width * 6,
            transcendentals=seqs * pairs * length * length,
        ),
        compiler_params=pltpu.CompilerParams(vmem_limit_bytes=60 << 20),
    )(qkv, context_grad, *tables)


def both_cores(core, rows, mine_ref, theirs_ref):
    yield pl.ds(pl.multiple_of(core * rows, rows), rows), mine_ref[0]
    yield pl.ds(pl.multiple_of((1 - core) * rows, rows), rows), theirs_ref[0]


def norm_kernel(core_ref, mine_ref, theirs_ref, gains_ref, one_ref, two_ref, normed_ref):
    for at, value in both_cores(core_ref[0], mine_ref.shape[1], mine_ref, theirs_ref):
        x = value.astype(F32)
        centred = x - jnp.mean(x, axis=-1, keepdims=True)
        normed = centred * lax.rsqrt(jnp.mean(centred * centred, axis=-1, keepdims=True) + epsilon)
        one_ref[at, :] = (normed * gains_ref[0:1, :] + gains_ref[1:2, :]).astype(BF)
        two_ref[at, :] = (normed * gains_ref[2:3, :] + gains_ref[3:4, :]).astype(BF)
        normed_ref[at, :] = normed.astype(BF)


def dy_kernel(core_ref, mine_ref, theirs_ref, dy_ref, sum_ref):
    @pl.when((pl.program_id(0) == 0) & (pl.program_id(1) == 0))
    def _():
        sum_ref[...] = jnp.zeros_like(sum_ref)

    sum_ref[...] += jnp.sum(mine_ref[0].astype(F32), 0, keepdims=True)
    for at, value in both_cores(core_ref[0], mine_ref.shape[1], mine_ref, theirs_ref):
        dy_ref[at, :] = value


def on_pairs(kernel, outputs, core, mine, theirs, per_chip, extra=(), sums=0):
    blocks, rows, width = mine.shape
    planes = blocks // per_chip
    source = pl.BlockSpec((1, rows, width), lambda s, p, core: (p * per_chip + s, 0, 0))
    target = pl.BlockSpec((2 * rows, width), lambda s, p, core: (s * planes + p, 0))
    shape = jax.ShapeDtypeStruct((2 * blocks * rows, width), BF)
    whole = [pl.BlockSpec(value.shape, lambda s, p, core: (0, 0)) for value in extra]
    return pl.pallas_call(
        kernel,
        out_shape=(shape,) * outputs + (jax.ShapeDtypeStruct((1, width), F32),) * sums,
        grid_spec=pltpu.PrefetchScalarGridSpec(
            num_scalar_prefetch=1,
            grid=(per_chip, planes),
            in_specs=[source, source] + whole,
            out_specs=(target,) * outputs
            + (pl.BlockSpec((1, width), lambda s, p, core: (0, 0)),) * sums,
        ),
        cost_estimate=pl.CostEstimate(
            flops=20 * blocks * rows * width,
            bytes_accessed=(4 + 4 * outputs) * blocks * rows * width,
            transcendentals=0,
        ),
    )(core.reshape(1), mine, theirs, *extra)


def weave(first_core, own, other, chips, hidden):
    rows = own.shape[0]
    block = hidden // chips

    def kernel(first_ref, own_ref, other_ref, out_ref):
        first = first_ref[0] == 1
        for chip in range(chips):
            here = slice(chip * block, (chip + 1) * block)
            mine, theirs = own_ref[:, here], other_ref[:, here]
            at = 2 * chip * block
            out_ref[:, at : at + block] = jnp.where(first, mine, theirs)
            out_ref[:, at + block : at + 2 * block] = jnp.where(first, theirs, mine)

    whole = pl.BlockSpec(memory_space=pltpu.VMEM)
    return pl.pallas_call(
        kernel,
        out_shape=jax.ShapeDtypeStruct((rows, 2 * hidden), own.dtype),
        in_specs=[pl.BlockSpec(memory_space=pltpu.SMEM), whole, whole],
        out_specs=whole,
    )(first_core.astype(jnp.int32).reshape(1), own, other)


def phi(u):
    density = jnp.exp(-0.5 * u * u) * (1.0 / math.sqrt(2.0 * math.pi))
    return 0.5 * (1.0 + lax.erf(u * math.sqrt(0.5))), density


def pipelined(chunks, first, second):
    ahead = first(chunks[0])
    for n, chunk in enumerate(chunks):
        following = first(chunks[n + 1]) if n + 1 < len(chunks) else None
        second(chunk, ahead)
        ahead = following


def starts(width, chunk=512):
    chunk = math.gcd(width, chunk)
    return [slice(at, at + chunk) for at in range(0, width, chunk)]


def stacked(ref, rows, cols):
    size = ref.shape[1]
    part = ref[rows.start // size : rows.stop // size, :, cols]
    return part.reshape(part.shape[0] * size, part.shape[2])


def shared_specs(shared):
    chips, rows, width = shared.shape
    low = pl.BlockSpec((chips, rows // 4, width), lambda *i: (0, 0, 0))
    high = pl.BlockSpec((chips, rows // 4, width), lambda *i: (0, 1, 0))
    down = pl.BlockSpec((chips, rows // 2, width), lambda *i: (0, 1, 0))
    return low, high, down


def up_kernel(a_ref, low_ref, high_ref, bias_ref, z_ref, slope_ref):
    width = low_ref.shape[2]
    everything = slice(0, a_ref.shape[1])
    a = a_ref[...]
    chunks = [
        (w_ref, here, slice(half * width + here.start, half * width + here.stop))
        for half, w_ref in enumerate((low_ref, high_ref))
        for here in starts(width, 256)
    ]

    def product(chunk):
        w_ref, here, there = chunk
        return dot_nn(a, stacked(w_ref, everything, here)) + bias_ref[:, there]

    def activate(chunk, u):
        there = chunk[2]
        cdf, density = phi(u)
        z_ref[:, there] = (u * cdf).astype(BF)
        slope_ref[:, there] = (cdf + u * density).astype(BF)

    pipelined(chunks, product, activate)


def up_project(a, shared, bias, block):
    count, width = a.shape
    hidden = bias.shape[1]
    low, high, _ = shared_specs(shared)
    wide = pl.BlockSpec((block, hidden), lambda i: (i, 0))
    shape = jax.ShapeDtypeStruct((count, hidden), BF)
    return pl.pallas_call(
        up_kernel,
        out_shape=(shape, shape),
        grid=(count // block,),
        in_specs=[
            pl.BlockSpec((block, width), lambda i: (i, 0)),
            low,
            high,
            pl.BlockSpec((1, hidden), lambda i: (0, 0)),
        ],
        out_specs=(wide, wide),
        cost_estimate=pl.CostEstimate(
            flops=2 * count * width * hidden,
            bytes_accessed=2 * (count * width + 2 * count * hidden + width * hidden),
            transcendentals=2 * count * hidden,
        ),
        compiler_params=pltpu.CompilerParams(vmem_limit_bytes=60 << 20),
    )(a, shared, shared, bias)


def dz_kernel(dy_ref, down_ref, slope_ref, du_ref, sum_ref):
    dy = dy_ref[...]
    everything = slice(0, dy.shape[1])

    @pl.when(pl.program_id(0) == 0)
    def _():
        sum_ref[...] = jnp.zeros_like(sum_ref)

    def product(here):
        return dot_nt(dy, stacked(down_ref, here, everything))

    def scale(here, dz):
        du = (dz * slope_ref[:, here].astype(F32)).astype(BF)
        du_ref[:, here] = du
        sum_ref[:, here] += jnp.sum(du.astype(F32), 0, keepdims=True)

    pipelined(starts(du_ref.shape[1]), product, scale)


def down_pull(dy, shared, slope, block):
    count, width = dy.shape
    hidden = slope.shape[1]
    wide = pl.BlockSpec((block, hidden), lambda i: (i, 0))
    return pl.pallas_call(
        dz_kernel,
        out_shape=(
            jax.ShapeDtypeStruct((count, hidden), BF),
            jax.ShapeDtypeStruct((1, hidden), F32),
        ),
        grid=(count // block,),
        in_specs=[
            pl.BlockSpec((block, width), lambda i: (i, 0)),
            shared_specs(shared)[2],
            wide,
        ],
        out_specs=(wide, pl.BlockSpec((1, hidden), lambda i: (0, 0))),
        cost_estimate=pl.CostEstimate(
            flops=2 * count * width * hidden,
            bytes_accessed=2 * (count * width + 2 * count * hidden + width * hidden),
            transcendentals=0,
        ),
        compiler_params=pltpu.CompilerParams(vmem_limit_bytes=60 << 20),
    )(dy, shared, slope)


def g_one_kernel(d_ref, w_ref, normed_ref, gain_ref, h_ref, sums_ref, bias_ref):
    @pl.when(pl.program_id(0) == 0)
    def _():
        sums_ref[...] = jnp.zeros_like(sums_ref)
        bias_ref[...] = jnp.zeros_like(bias_ref)

    d = d_ref[...]

    def product(here):
        return dot_nt(d, w_ref[here, :])

    def scale(here, g):
        h_ref[:, here] = (g * gain_ref[:, here]).astype(BF)
        sums_ref[0:1, here] += jnp.sum(g * normed_ref[:, here].astype(F32), 0, keepdims=True)
        sums_ref[1:2, here] += jnp.sum(g, 0, keepdims=True)

    pipelined(starts(h_ref.shape[1]), product, scale)
    bias_ref[...] += jnp.sum(d.astype(F32), 0, keepdims=True)


def pull_one(d, weights, normed, gain, block):
    count, inner = d.shape
    width = gain.shape[1]
    return pl.pallas_call(
        g_one_kernel,
        out_shape=(
            jax.ShapeDtypeStruct((count, width), BF),
            jax.ShapeDtypeStruct((2, width), F32),
            jax.ShapeDtypeStruct((1, inner), F32),
        ),
        grid=(count // block,),
        in_specs=[
            pl.BlockSpec((block, inner), lambda i: (i, 0)),
            pl.BlockSpec((width, inner), lambda i: (0, 0)),
            pl.BlockSpec((block, width), lambda i: (i, 0)),
            pl.BlockSpec((1, width), lambda i: (0, 0)),
        ],
        out_specs=(
            pl.BlockSpec((block, width), lambda i: (i, 0)),
            pl.BlockSpec((2, width), lambda i: (0, 0)),
            pl.BlockSpec((1, inner), lambda i: (0, 0)),
        ),
        cost_estimate=pl.CostEstimate(
            flops=2 * count * width * inner,
            bytes_accessed=2 * count * (inner + 2 * width),
            transcendentals=0,
        ),
        compiler_params=pltpu.CompilerParams(vmem_limit_bytes=60 << 20),
    )(d, weights, normed, gain)


def split_rows(core, value_ref, kept_ref, sent_ref, cols, extra):
    planes, _, rows, _ = kept_ref.shape
    for p in range(planes):
        own = pl.ds(pl.multiple_of((2 * p + core) * rows, rows), rows)
        other = pl.ds(pl.multiple_of((2 * p + 1 - core) * rows, rows), rows)
        kept = value_ref[own, :]
        kept_ref[p, 0, :, cols] = kept if extra is None else kept + extra(p)
        sent_ref[p, 0, :, cols] = value_ref[other, :].astype(BF)


def g_two_kernel(
    core_ref,
    d_ref,
    low_ref,
    high_ref,
    normed_ref,
    gain_ref,
    h_ref,
    kept_ref,
    sent_ref,
    sums_ref,
    value_s,
):
    @pl.when((pl.program_id(0) == 0) & (pl.program_id(1) == 0))
    def _():
        sums_ref[...] = jnp.zeros_like(sums_ref)

    width = low_ref.shape[2]
    everything = slice(0, width)

    def product(here):
        return dot_nt(d_ref[:, :width], stacked(low_ref, here, everything)) + dot_nt(
            d_ref[:, width:], stacked(high_ref, here, everything)
        )

    def scale(here, g):
        value_s[...] = g * gain_ref[:, here] + h_ref[:, here].astype(F32)
        sums_ref[0:1, here] += jnp.sum(g * normed_ref[:, here].astype(F32), 0, keepdims=True)
        sums_ref[1:2, here] += jnp.sum(g, 0, keepdims=True)
        split_rows(core_ref[0], value_s, kept_ref, sent_ref, here, None)

    pipelined(starts(width), product, scale)


def token_specs(planes, per_chip, rows, width, group):
    full = planes // group
    piece = pl.BlockSpec((group, 1, rows, width), lambda s, p, core: (p, s, 0, 0))

    def block(cols):
        return pl.BlockSpec((2 * group * rows, cols), lambda s, p, core: (s * full + p, 0))

    return (per_chip, full), piece, block


def pull_two(core, d, shared, normed, gain, h_one, planes, per_chip, rows):
    count, inner = d.shape
    width = gain.shape[1]
    group = math.gcd(planes, 2)
    grid, piece, block = token_specs(planes, per_chip, rows, width, group)
    low, high, _ = shared_specs(shared)
    shape = (planes, per_chip, rows, width)
    return pl.pallas_call(
        g_two_kernel,
        out_shape=(
            jax.ShapeDtypeStruct(shape, F32),
            jax.ShapeDtypeStruct(shape, BF),
            jax.ShapeDtypeStruct((2, width), F32),
        ),
        grid_spec=pltpu.PrefetchScalarGridSpec(
            num_scalar_prefetch=1,
            grid=grid,
            in_specs=[
                block(inner),
                low,
                high,
                block(width),
                pl.BlockSpec((1, width), lambda s, p, core: (0, 0)),
                block(width),
            ],
            out_specs=(piece, piece, pl.BlockSpec((2, width), lambda s, p, core: (0, 0))),
            scratch_shapes=[pltpu.VMEM((2 * group * rows, math.gcd(width, 512)), F32)],
        ),
        cost_estimate=pl.CostEstimate(
            flops=2 * count * width * inner,
            bytes_accessed=2 * count * (inner + 4 * width),
            transcendentals=0,
        ),
        compiler_params=pltpu.CompilerParams(vmem_limit_bytes=60 << 20),
    )(core.reshape(1), d, shared, shared, normed, gain, h_one)


def out_kernel(
    core_ref, z_ref, down_ref, ctx_ref, out_ref, x_ref, bias_ref, kept_ref, sent_ref, value_s
):
    def product(here):
        down = stacked(down_ref, slice(0, z_ref.shape[1]), here)
        return dot_nn(z_ref[...], down) + dot_nn(ctx_ref[...], out_ref[:, here])

    def split(here, value):
        value_s[...] = value
        split_rows(
            core_ref[0],
            value_s,
            kept_ref,
            sent_ref,
            here,
            lambda p: x_ref[p, 0, :, here].astype(F32) + bias_ref[:, here],
        )

    pipelined(starts(out_ref.shape[1]), product, split)


def out_project(core, z, shared, context, w_out, x_mine, bias, planes, per_chip, rows):
    count, hidden = z.shape
    inner, width = w_out.shape
    group = math.gcd(planes, 2)
    grid, piece, block = token_specs(planes, per_chip, rows, width, group)
    shape = (planes, per_chip, rows, width)
    return pl.pallas_call(
        out_kernel,
        out_shape=(jax.ShapeDtypeStruct(shape, F32), jax.ShapeDtypeStruct(shape, BF)),
        grid_spec=pltpu.PrefetchScalarGridSpec(
            num_scalar_prefetch=1,
            grid=grid,
            in_specs=[
                block(hidden),
                shared_specs(shared)[2],
                block(inner),
                pl.BlockSpec((inner, width), lambda s, p, core: (0, 0)),
                piece,
                pl.BlockSpec((1, width), lambda s, p, core: (0, 0)),
            ],
            out_specs=(piece, piece),
            scratch_shapes=[pltpu.VMEM((2 * group * rows, math.gcd(width, 512)), F32)],
        ),
        cost_estimate=pl.CostEstimate(
            flops=2 * count * width * (hidden + inner),
            bytes_accessed=2 * count * (hidden + inner + 4 * width),
            transcendentals=0,
        ),
        compiler_params=pltpu.CompilerParams(vmem_limit_bytes=60 << 20),
    )(core.reshape(1), z, shared, context, w_out, x_mine.reshape(shape), bias)


def ordered(value, *before):
    return lax.optimization_barrier((value,) + before)[0]


def local(
    tokens,
    ln1_gain,
    ln1_shift,
    ln2_gain,
    ln2_shift,
    qkv_weight,
    qkv_bias,
    out_weight,
    out_bias,
    in_weight,
    in_bias,
    down_weight,
    down_bias,
    cotangent,
):
    planes = lax.axis_size("pl")
    chips = lax.axis_size("dp") * planes
    n = 2 * chips
    core = lax.axis_index("core")
    first_core = core == 0
    seqs, rows_here, width = tokens.shape
    per_chip = seqs // planes
    length = rows_here * planes * 2
    count = per_chip * length
    heads = H // 2
    qkv_cols = heads * 3 * HD
    ctx_cols = heads * HD
    hidden = in_weight.shape[1] // 2
    own_rows = qkv_weight.shape[0]

    def swap(value, mask):
        return lax.ppermute(value, AXES, [(i, i ^ mask) for i in range(n)])

    def in_core_order(own, other, axis):
        return jnp.where(
            first_core, jnp.concatenate([own, other], axis), jnp.concatenate([other, own], axis)
        )

    def pick(value, index, axis):
        return lax.dynamic_index_in_dim(value, index, axis, keepdims=False)

    qkv_halves = (
        qkv_weight.reshape(own_rows, 2, heads // 2, 2, 3, HD)
        .transpose(1, 0, 2, 4, 3, 5)
        .reshape(2, own_rows, qkv_cols)
    )
    out_halves = out_weight.reshape(own_rows, 2, ctx_cols).transpose(1, 0, 2)
    in_halves = (
        in_weight.reshape(own_rows, chips, 2, hidden // chips)
        .transpose(2, 0, 1, 3)
        .reshape(2, own_rows, hidden)
    )
    halves = jnp.concatenate([qkv_halves, out_halves, in_halves], 2)
    chip_rows = in_core_order(pick(halves, core, 0), swap(pick(halves, 1 - core, 0), 1), 0)
    first_cols = qkv_cols + ctx_cols
    first_all = lax.all_gather(chip_rows[:, :first_cols], CHIPS, axis=0, tiled=True)
    small = jnp.concatenate(
        [ln1_gain, ln1_shift, ln2_gain, ln2_shift, out_bias, down_bias, qkv_bias, in_bias]
    )
    small = jnp.broadcast_to(small[None, :], (n, small.shape[0]))
    small = ordered(small, chip_rows)
    small = lax.all_to_all(small, AXES, split_axis=0, concat_axis=0, tiled=True)
    small = small.astype(F32)
    part = width // n
    gain_one, shift_one, gain_two, shift_two, b_out, b_down = (
        small[:, i * part : (i + 1) * part].reshape(width) for i in range(6)
    )
    b_qkv = small[:, 6 * part : 9 * part].reshape(2, heads // 2, 2, 3, HD)
    b_qkv = pick(b_qkv, core, 0).transpose(0, 2, 1, 3).reshape(qkv_cols)
    b_in = pick(small[:, 9 * part :].reshape(chips, 2, hidden // chips), core, 1).reshape(hidden)

    deep = chips // planes
    second = jnp.concatenate(
        [
            chip_rows[:, first_cols : first_cols + width],
            chip_rows[:, first_cols + width :],
            down_weight,
        ],
        0,
    )
    shared = lax.all_gather(second[None], CHIPS, axis=0, tiled=True)
    other_rows = lax.dynamic_slice(first_all, ((1 - core) * ctx_cols, qkv_cols), (ctx_cols, ctx_cols))
    some_rows = lax.dynamic_slice(first_all, (core * ctx_cols, qkv_cols), (ctx_cols, ctx_cols))
    w_out = in_core_order(some_rows, swap(other_rows, 1), 1)
    w_qkv = first_all[:, :qkv_cols]

    def to_chip(value):
        mine = lax.all_to_all(value, "pl", split_axis=0, concat_axis=0, tiled=True)
        return mine, swap(mine, 1)

    def to_tokens(kept, sent):
        value = (kept + swap(sent, 1).astype(F32)).astype(BF)
        value = value.reshape(seqs, rows_here, width)
        return lax.all_to_all(value, "pl", split_axis=0, concat_axis=0, tiled=True)

    x_mine, x_theirs = to_chip(ordered(tokens, chip_rows))
    dy_mine, dy_theirs = to_chip(ordered(cotangent, x_mine))
    gains = jnp.stack([gain_one, shift_one, gain_two, shift_two])
    dy, dy_sum = on_pairs(dy_kernel, 1, core, dy_mine, dy_theirs, per_chip, sums=1)
    a_one, a_two, normed = on_pairs(
        norm_kernel, 3, core, x_mine, x_theirs, per_chip, (gains,)
    )

    qkv = (dot_nn(a_one, w_qkv) + b_qkv).astype(BF)
    context_grad = dot_nt(dy, w_out).astype(BF)
    context, qkv_grad = attention(
        qkv.reshape(per_chip, length, qkv_cols),
        context_grad.reshape(per_chip, length, ctx_cols),
        rotary_lanes(length),
    )
    context = context.reshape(count, ctx_cols)
    qkv_grad = qkv_grad.reshape(count, qkv_cols)

    plane_here = lax.axis_index("pl")
    deep_here = lax.axis_index("dp")

    def direct_sum(value, axis, size, here, stride, final):
        total = pick(value, here, axis).astype(F32)
        for k in range(1, size):
            total += swap(pick(value, here ^ k, axis), k * stride).astype(F32)
        return total if final else total.astype(BF)

    def plane_then_deep(value):
        value = value.reshape(deep, planes, value.shape[0] // chips, value.shape[1])
        value = direct_sum(value, 1, planes, plane_here, 2, False)
        return direct_sum(value, 0, deep, deep_here, 2 * planes, True)

    def deep_then_plane(value):
        value = value.reshape(deep, planes, value.shape[0] // chips, value.shape[1])
        value = direct_sum(value, 0, deep, deep_here, 2 * planes, False)
        return direct_sum(value, 0, planes, plane_here, 2, True)

    def own_rows_of(value):
        value = value.reshape(2, own_rows, value.shape[1])
        return pick(value, core, 0), swap(pick(value, 1 - core, 0), 1)

    out_w_grad = dot_tn(context, dy).astype(BF)
    other_cols = lax.dynamic_slice_in_dim(out_w_grad, (1 - core) * ctx_cols, ctx_cols, 1)
    own_cols = lax.dynamic_slice_in_dim(out_w_grad, core * ctx_cols, ctx_cols, 1)
    out_w_grad = in_core_order(own_cols, swap(other_cols, 1), 0)
    qkv_w_grad = dot_tn(a_one, qkv_grad).astype(BF)
    first_grad = jnp.concatenate([qkv_w_grad, out_w_grad], 1)
    first_grad = first_grad.reshape(deep, planes, 2 * own_rows, first_cols).transpose(1, 0, 2, 3)
    first_grad = lax.all_to_all(first_grad, "pl", split_axis=0, concat_axis=0, tiled=True)
    first_grad = jnp.sum(first_grad.astype(F32), 0).astype(BF)
    first_grad = direct_sum(first_grad, 0, deep, deep_here, 2 * planes, True)
    first_own, first_other = own_rows_of(first_grad)
    first_grad = in_core_order(first_own[:, None], first_other[:, None], 1)
    qkv_w_grad = (
        first_grad[:, :, :qkv_cols]
        .reshape(own_rows, 2, heads // 2, 3, 2, HD)
        .transpose(0, 1, 2, 4, 3, 5)
        .reshape(own_rows, 2 * qkv_cols)
    )
    out_w_grad = first_grad[:, :, qkv_cols:].reshape(own_rows, width)
    block = math.gcd(count, 512)
    h_one, sums_one, qkv_b_grad = pull_one(qkv_grad, first_all, normed, gain_one[None], block)

    qkv_b_grad = (
        qkv_b_grad.reshape(heads // 2, 3, 2, HD).transpose(0, 2, 1, 3).reshape(qkv_cols)
    )
    qkv_b_grad = in_core_order(qkv_b_grad, jnp.zeros_like(qkv_b_grad), 0)
    sums = [sums_one[0], sums_one[1], dy_sum, qkv_b_grad]
    sums = jnp.concatenate([value.reshape(n, -1) for value in sums], 1)
    sums = lax.all_to_all(sums, AXES, split_axis=0, concat_axis=0, tiled=True)
    sums = jnp.sum(sums, 0)

    z, slope = up_project(a_two, shared, b_in[None], block)
    down_w_grad = dot_tn(z, dy).astype(BF)
    down_w_grad = plane_then_deep(down_w_grad)
    du, in_b_grad = down_pull(dy, shared, slope, block)
    in_w_grad = dot_tn(a_two, du).astype(BF)
    kept, sent, sums_two = pull_two(
        core, du, shared, normed, gain_two[None], h_one, planes, per_chip, rows_here
    )
    combined = to_tokens(kept, sent)
    per_row = hidden // width
    riders = jnp.concatenate(
        [sums_two.T, in_b_grad.reshape(width, per_row), jnp.zeros((width, PAIR - 2 - per_row), F32)], 1
    )
    in_w_grad = jnp.concatenate(
        [
            plane_then_deep(in_w_grad[:, : 3 * hidden // 4]),
            deep_then_plane(
                jnp.concatenate([in_w_grad[:, 3 * hidden // 4 :], riders.astype(BF)], 1)
            ),
        ],
        1,
    )
    in_b_grad = in_w_grad[:, hidden + 2 : hidden + 2 + per_row].reshape(hidden // chips)
    in_w_own, in_w_other = own_rows_of(in_w_grad)
    ln2_grads = (in_w_own + in_w_other)[:, hidden : hidden + 2]
    in_w_grad = weave(first_core, in_w_own, in_w_other, chips, hidden)
    kept, sent = out_project(
        core, z, shared, context, w_out, x_mine, (b_out + b_down)[None], planes, per_chip, rows_here
    )
    output = to_tokens(kept, sent)

    x_here = tokens.astype(F32)
    mean_here = jnp.mean(x_here, axis=-1, keepdims=True)
    centred_here = x_here - mean_here
    scale_here = lax.rsqrt(jnp.mean(centred_here * centred_here, axis=-1, keepdims=True) + epsilon)
    normed_here = centred_here * scale_here
    combined = combined.astype(F32)
    pulled = (
        combined
        - jnp.mean(combined, axis=-1, keepdims=True)
        - normed_here * jnp.mean(combined * normed_here, axis=-1, keepdims=True)
    ) * scale_here
    dy_here = cotangent.astype(F32)
    input_grad = dy_here + pulled

    b_grad = sums[2 * part : 3 * part]
    return (
        output,
        input_grad,
        sums[:part],
        sums[part : 2 * part],
        ln2_grads[:, 0],
        ln2_grads[:, 1],
        qkv_w_grad,
        sums[3 * part :],
        out_w_grad,
        b_grad,
        in_w_grad,
        in_b_grad,
        down_w_grad,
        b_grad,
    )


def solution(mesh):
    split = Mesh(
        mesh.devices.reshape(mesh.shape["dp"], mesh.shape["seq"] // 2, 2),
        AXES,
    )
    rows = P("dp", ("pl", "core"), None)
    vector = P(AXES)
    matrix = P(AXES, None)
    return jax.shard_map(
        local,
        mesh=split,
        in_specs=(
            rows,
            vector,
            vector,
            vector,
            vector,
            matrix,
            vector,
            matrix,
            vector,
            matrix,
            vector,
            matrix,
            vector,
            rows,
        ),
        out_specs=(
            rows,
            rows,
            vector,
            vector,
            vector,
            vector,
            matrix,
            vector,
            matrix,
            vector,
            matrix,
            vector,
            matrix,
            vector,
        ),
        check_vma=False,
    )
```

```python
import functools
import math

import jax
import jax.numpy as jnp
from jax import lax
from jax.experimental import pallas as pl
from jax.experimental.pallas import tpu as pltpu
from jax.sharding import Mesh
from jax.sharding import PartitionSpec as P


H = 16
HD = 64
ROT = 16
PAIR = 2 * HD
AXES = ("dp", "pl", "core")
CHIPS = ("dp", "pl")
BF = jnp.bfloat16
F32 = jnp.float32

epsilon = 1e-05


def dot_nn(left, right):
    return lax.dot_general(left, right, (((1,), (0,)), ((), ())), preferred_element_type=F32)


def dot_nt(left, right):
    return lax.dot_general(left, right, (((1,), (1,)), ((), ())), preferred_element_type=F32)


def dot_tn(left, right):
    return lax.dot_general(left, right, (((0,), (0,)), ((), ())), preferred_element_type=F32)


def rotary_lanes(length):
    lane = jnp.arange(PAIR, dtype=jnp.int32) % HD
    half = ROT // 2
    inverse = jnp.exp((lane % half).astype(F32) * (-2.0 * math.log(10000.0) / ROT))
    angles = jnp.arange(length, dtype=F32)[:, None] * inverse[None, :]
    turned = (lane < ROT)[None, :]
    first = (lane < half)[None, :]
    sines = jnp.sin(angles)
    return (
        jnp.where(turned, jnp.cos(angles), 1.0),
        jnp.where(first, -sines, 0.0),
        jnp.where(turned & ~first, sines, 0.0),
    )


def attention_kernel(
    block,
    qkv_ref,
    dc_ref,
    cos_ref,
    sin_a_ref,
    sin_b_ref,
    ctx_ref,
    dqkv_ref,
    q_s,
    k_s,
    kt_s,
    vt_s,
    ctxt_s,
    dqt_s,
    dk_s,
    dv_s,
):
    length = qkv_ref.shape[1]
    half = ROT // 2
    factor = 1.0 / math.sqrt(HD)
    value_cols = slice(2 * PAIR, 3 * PAIR)

    def turn(z, sign):
        swapped = pltpu.roll(z, PAIR - half, 1) * sin_a_ref[...] + pltpu.roll(z, half, 1) * sin_b_ref[...]
        return z * cos_ref[...] + sign * swapped

    q_s[...] = turn(qkv_ref[0, :, 0:PAIR].astype(F32), 1.0).astype(BF) * BF(factor)
    keys = turn(qkv_ref[0, :, PAIR : 2 * PAIR].astype(F32), 1.0).astype(BF)
    k_s[...] = keys
    kt_s[...] = keys.T
    vt_s[...] = qkv_ref[0, :, value_cols].T
    dk_s[...] = jnp.zeros_like(dk_s)
    dv_s[...] = jnp.zeros_like(dv_s)
    lane = lax.broadcasted_iota(jnp.int32, (1, PAIR), 1)
    keys_at = lax.broadcasted_iota(jnp.int32, (block, block), 0)
    queries_at = lax.broadcasted_iota(jnp.int32, (block, block), 1)
    chosen = [((lane >= h * HD) & (lane < h * HD + HD)).astype(BF) for h in range(2)]

    def front(h, i):
        lo, hi = i * block, (i + 1) * block
        queries = q_s[lo:hi, :] * chosen[h]
        grads = dc_ref[0, lo:hi, :] * chosen[h]
        scores = dot_nt(k_s[0:hi, :], queries)
        return scores, dot_nt(qkv_ref[0, 0:hi, value_cols], grads), queries, grads

    def middle(i, scores, weight_grad, queries, grads):
        lo, hi = i * block, (i + 1) * block
        last = jnp.where(keys_at <= queries_at, scores[lo:hi, :], -1e30)
        scores = jnp.concatenate([scores[:lo, :], last], 0) if i else last
        weights = jnp.exp(scores - jnp.max(scores, axis=0, keepdims=True))
        weights = weights * (1.0 / jnp.sum(weights, axis=0, keepdims=True))
        mixed = jnp.sum(weights * weight_grad, axis=0, keepdims=True)
        score_grad = (weights * (weight_grad - mixed)).astype(BF)
        return weights.astype(BF), score_grad, queries, grads

    def back(h, i, weights, score_grad, queries, grads):
        lo, hi = i * block, (i + 1) * block
        dims = slice(h * HD, h * HD + HD)
        ctxt_s[dims, lo:hi] = dot_nn(vt_s[dims, 0:hi], weights)
        dv_s[0:hi, :] += dot_nn(weights, grads)
        dk_s[0:hi, :] += dot_nn(score_grad, queries)
        dqt_s[dims, lo:hi] = dot_nn(kt_s[dims, 0:hi], score_grad)

    order = [(h, i) for i in range(length // block) for h in range(2)]
    ahead = front(*order[0])
    behind = None
    for step, (h, i) in enumerate(order):
        following = front(*order[step + 1]) if step + 1 < len(order) else None
        results = middle(i, *ahead)
        if behind is not None:
            back(*behind)
        behind = (h, i, *results)
        ahead = following
    back(*behind)
    ctx_ref[0] = ctxt_s[...].T.astype(BF)
    dqkv_ref[0, :, 0:PAIR] = turn(dqt_s[...].T * factor, -1.0).astype(BF)
    dqkv_ref[0, :, PAIR : 2 * PAIR] = turn(dk_s[...], -1.0).astype(BF)
    dqkv_ref[0, :, value_cols] = dv_s[...].astype(BF)


def attention(qkv, context_grad, tables):
    seqs, length, width = qkv.shape
    pairs = width // (3 * PAIR)
    table = pl.BlockSpec((length, PAIR), lambda s, h: (0, 0))
    wide = pl.BlockSpec((1, length, 3 * PAIR), lambda s, h: (s, 0, h))
    slim = pl.BlockSpec((1, length, PAIR), lambda s, h: (s, 0, h))
    return pl.pallas_call(
        functools.partial(attention_kernel, math.gcd(length, 256)),
        out_shape=(
            jax.ShapeDtypeStruct((seqs, length, width // 3), BF),
            jax.ShapeDtypeStruct((seqs, length, width), BF),
        ),
        grid=(seqs, pairs),
        in_specs=[wide, slim, table, table, table],
        out_specs=(slim, wide),
        scratch_shapes=[pltpu.VMEM((length, PAIR), BF)] * 2
        + [pltpu.VMEM((PAIR, length), BF)] * 2
        + [pltpu.VMEM((PAIR, length), F32)] * 2
        + [pltpu.VMEM((length, PAIR), F32)] * 2,
        cost_estimate=pl.CostEstimate(
            flops=seqs * pairs * 2 * 7 * length * length * PAIR,
            bytes_accessed=seqs * length * width * 6,
            transcendentals=seqs * pairs * length * length,
        ),
        compiler_params=pltpu.CompilerParams(vmem_limit_bytes=60 << 20),
    )(qkv, context_grad, *tables)


def both_cores(core, rows, mine_ref, theirs_ref):
    yield pl.ds(pl.multiple_of(core * rows, rows), rows), mine_ref[0]
    yield pl.ds(pl.multiple_of((1 - core) * rows, rows), rows), theirs_ref[0]


def norm_kernel(core_ref, mine_ref, theirs_ref, gains_ref, one_ref, two_ref, normed_ref):
    for at, value in both_cores(core_ref[0], mine_ref.shape[1], mine_ref, theirs_ref):
        x = value.astype(F32)
        centred = x - jnp.mean(x, axis=-1, keepdims=True)
        normed = centred * lax.rsqrt(jnp.mean(centred * centred, axis=-1, keepdims=True) + epsilon)
        one_ref[at, :] = (normed * gains_ref[0:1, :] + gains_ref[1:2, :]).astype(BF)
        two_ref[at, :] = (normed * gains_ref[2:3, :] + gains_ref[3:4, :]).astype(BF)
        normed_ref[at, :] = normed.astype(BF)


def dy_kernel(core_ref, mine_ref, theirs_ref, dy_ref, sum_ref):
    @pl.when((pl.program_id(0) == 0) & (pl.program_id(1) == 0))
    def _():
        sum_ref[...] = jnp.zeros_like(sum_ref)

    sum_ref[...] += jnp.sum(mine_ref[0].astype(F32), 0, keepdims=True)
    for at, value in both_cores(core_ref[0], mine_ref.shape[1], mine_ref, theirs_ref):
        dy_ref[at, :] = value


def on_pairs(kernel, outputs, core, mine, theirs, per_chip, extra=(), sums=0):
    blocks, rows, width = mine.shape
    planes = blocks // per_chip
    source = pl.BlockSpec((1, rows, width), lambda s, p, core: (p * per_chip + s, 0, 0))
    target = pl.BlockSpec((2 * rows, width), lambda s, p, core: (s * planes + p, 0))
    shape = jax.ShapeDtypeStruct((2 * blocks * rows, width), BF)
    whole = [pl.BlockSpec(value.shape, lambda s, p, core: (0, 0)) for value in extra]
    return pl.pallas_call(
        kernel,
        out_shape=(shape,) * outputs + (jax.ShapeDtypeStruct((1, width), F32),) * sums,
        grid_spec=pltpu.PrefetchScalarGridSpec(
            num_scalar_prefetch=1,
            grid=(per_chip, planes),
            in_specs=[source, source] + whole,
            out_specs=(target,) * outputs
            + (pl.BlockSpec((1, width), lambda s, p, core: (0, 0)),) * sums,
        ),
        cost_estimate=pl.CostEstimate(
            flops=20 * blocks * rows * width,
            bytes_accessed=(4 + 4 * outputs) * blocks * rows * width,
            transcendentals=0,
        ),
    )(core.reshape(1), mine, theirs, *extra)


def weave(first_core, own, other, chips, hidden):
    rows = own.shape[0]
    block = hidden // chips

    def kernel(first_ref, own_ref, other_ref, out_ref):
        first = first_ref[0] == 1
        for chip in range(chips):
            here = slice(chip * block, (chip + 1) * block)
            mine, theirs = own_ref[:, here], other_ref[:, here]
            at = 2 * chip * block
            out_ref[:, at : at + block] = jnp.where(first, mine, theirs)
            out_ref[:, at + block : at + 2 * block] = jnp.where(first, theirs, mine)

    whole = pl.BlockSpec(memory_space=pltpu.VMEM)
    return pl.pallas_call(
        kernel,
        out_shape=jax.ShapeDtypeStruct((rows, 2 * hidden), own.dtype),
        in_specs=[pl.BlockSpec(memory_space=pltpu.SMEM), whole, whole],
        out_specs=whole,
    )(first_core.astype(jnp.int32).reshape(1), own, other)


def phi(u):
    density = jnp.exp(-0.5 * u * u) * (1.0 / math.sqrt(2.0 * math.pi))
    return 0.5 * (1.0 + lax.erf(u * math.sqrt(0.5))), density


def pipelined(chunks, first, second):
    ahead = first(chunks[0])
    for n, chunk in enumerate(chunks):
        following = first(chunks[n + 1]) if n + 1 < len(chunks) else None
        second(chunk, ahead)
        ahead = following


def starts(width, chunk=512):
    chunk = math.gcd(width, chunk)
    return [slice(at, at + chunk) for at in range(0, width, chunk)]


def stacked(ref, rows, cols):
    size = ref.shape[1]
    part = ref[rows.start // size : rows.stop // size, :, cols]
    return part.reshape(part.shape[0] * size, part.shape[2])


def shared_specs(shared):
    chips, rows, width = shared.shape
    low = pl.BlockSpec((chips, rows // 4, width), lambda *i: (0, 0, 0))
    high = pl.BlockSpec((chips, rows // 4, width), lambda *i: (0, 1, 0))
    down = pl.BlockSpec((chips, rows // 2, width), lambda *i: (0, 1, 0))
    return low, high, down


def up_kernel(a_ref, low_ref, high_ref, bias_ref, z_ref, slope_ref):
    width = low_ref.shape[2]
    everything = slice(0, a_ref.shape[1])
    a = a_ref[...]
    chunks = [
        (w_ref, here, slice(half * width + here.start, half * width + here.stop))
        for half, w_ref in enumerate((low_ref, high_ref))
        for here in starts(width, 256)
    ]

    def product(chunk):
        w_ref, here, there = chunk
        return dot_nn(a, stacked(w_ref, everything, here)) + bias_ref[:, there]

    def activate(chunk, u):
        there = chunk[2]
        cdf, density = phi(u)
        z_ref[:, there] = (u * cdf).astype(BF)
        slope_ref[:, there] = (cdf + u * density).astype(BF)

    pipelined(chunks, product, activate)


def up_project(a, shared, bias, block):
    count, width = a.shape
    hidden = bias.shape[1]
    low, high, _ = shared_specs(shared)
    wide = pl.BlockSpec((block, hidden), lambda i: (i, 0))
    shape = jax.ShapeDtypeStruct((count, hidden), BF)
    return pl.pallas_call(
        up_kernel,
        out_shape=(shape, shape),
        grid=(count // block,),
        in_specs=[
            pl.BlockSpec((block, width), lambda i: (i, 0)),
            low,
            high,
            pl.BlockSpec((1, hidden), lambda i: (0, 0)),
        ],
        out_specs=(wide, wide),
        cost_estimate=pl.CostEstimate(
            flops=2 * count * width * hidden,
            bytes_accessed=2 * (count * width + 2 * count * hidden + width * hidden),
            transcendentals=2 * count * hidden,
        ),
        compiler_params=pltpu.CompilerParams(vmem_limit_bytes=60 << 20),
    )(a, shared, shared, bias)


def dz_kernel(dy_ref, down_ref, slope_ref, du_ref, sum_ref):
    dy = dy_ref[...]
    everything = slice(0, dy.shape[1])

    @pl.when(pl.program_id(0) == 0)
    def _():
        sum_ref[...] = jnp.zeros_like(sum_ref)

    def product(here):
        return dot_nt(dy, stacked(down_ref, here, everything))

    def scale(here, dz):
        du = (dz * slope_ref[:, here].astype(F32)).astype(BF)
        du_ref[:, here] = du
        sum_ref[:, here] += jnp.sum(du.astype(F32), 0, keepdims=True)

    pipelined(starts(du_ref.shape[1]), product, scale)


def down_pull(dy, shared, slope, block):
    count, width = dy.shape
    hidden = slope.shape[1]
    wide = pl.BlockSpec((block, hidden), lambda i: (i, 0))
    return pl.pallas_call(
        dz_kernel,
        out_shape=(
            jax.ShapeDtypeStruct((count, hidden), BF),
            jax.ShapeDtypeStruct((1, hidden), F32),
        ),
        grid=(count // block,),
        in_specs=[
            pl.BlockSpec((block, width), lambda i: (i, 0)),
            shared_specs(shared)[2],
            wide,
        ],
        out_specs=(wide, pl.BlockSpec((1, hidden), lambda i: (0, 0))),
        cost_estimate=pl.CostEstimate(
            flops=2 * count * width * hidden,
            bytes_accessed=2 * (count * width + 2 * count * hidden + width * hidden),
            transcendentals=0,
        ),
        compiler_params=pltpu.CompilerParams(vmem_limit_bytes=60 << 20),
    )(dy, shared, slope)


def g_one_kernel(d_ref, w_ref, normed_ref, gain_ref, h_ref, sums_ref, bias_ref):
    @pl.when(pl.program_id(0) == 0)
    def _():
        sums_ref[...] = jnp.zeros_like(sums_ref)
        bias_ref[...] = jnp.zeros_like(bias_ref)

    d = d_ref[...]

    def product(here):
        return dot_nt(d, w_ref[here, :])

    def scale(here, g):
        h_ref[:, here] = (g * gain_ref[:, here]).astype(BF)
        sums_ref[0:1, here] += jnp.sum(g * normed_ref[:, here].astype(F32), 0, keepdims=True)
        sums_ref[1:2, here] += jnp.sum(g, 0, keepdims=True)

    pipelined(starts(h_ref.shape[1]), product, scale)
    bias_ref[...] += jnp.sum(d.astype(F32), 0, keepdims=True)


def pull_one(d, weights, normed, gain, block):
    count, inner = d.shape
    width = gain.shape[1]
    return pl.pallas_call(
        g_one_kernel,
        out_shape=(
            jax.ShapeDtypeStruct((count, width), BF),
            jax.ShapeDtypeStruct((2, width), F32),
            jax.ShapeDtypeStruct((1, inner), F32),
        ),
        grid=(count // block,),
        in_specs=[
            pl.BlockSpec((block, inner), lambda i: (i, 0)),
            pl.BlockSpec((width, inner), lambda i: (0, 0)),
            pl.BlockSpec((block, width), lambda i: (i, 0)),
            pl.BlockSpec((1, width), lambda i: (0, 0)),
        ],
        out_specs=(
            pl.BlockSpec((block, width), lambda i: (i, 0)),
            pl.BlockSpec((2, width), lambda i: (0, 0)),
            pl.BlockSpec((1, inner), lambda i: (0, 0)),
        ),
        cost_estimate=pl.CostEstimate(
            flops=2 * count * width * inner,
            bytes_accessed=2 * count * (inner + 2 * width),
            transcendentals=0,
        ),
        compiler_params=pltpu.CompilerParams(vmem_limit_bytes=60 << 20),
    )(d, weights, normed, gain)


def split_rows(core, value_ref, kept_ref, sent_ref, cols, extra):
    planes, _, rows, _ = kept_ref.shape
    for p in range(planes):
        own = pl.ds(pl.multiple_of((2 * p + core) * rows, rows), rows)
        other = pl.ds(pl.multiple_of((2 * p + 1 - core) * rows, rows), rows)
        kept = value_ref[own, :]
        kept_ref[p, 0, :, cols] = kept if extra is None else kept + extra(p)
        sent_ref[p, 0, :, cols] = value_ref[other, :].astype(BF)


def g_two_kernel(
    core_ref,
    d_ref,
    low_ref,
    high_ref,
    normed_ref,
    gain_ref,
    h_ref,
    kept_ref,
    sent_ref,
    sums_ref,
    value_s,
):
    @pl.when((pl.program_id(0) == 0) & (pl.program_id(1) == 0))
    def _():
        sums_ref[...] = jnp.zeros_like(sums_ref)

    width = low_ref.shape[2]
    everything = slice(0, width)

    def product(here):
        return dot_nt(d_ref[:, :width], stacked(low_ref, here, everything)) + dot_nt(
            d_ref[:, width:], stacked(high_ref, here, everything)
        )

    def scale(here, g):
        value_s[...] = g * gain_ref[:, here] + h_ref[:, here].astype(F32)
        sums_ref[0:1, here] += jnp.sum(g * normed_ref[:, here].astype(F32), 0, keepdims=True)
        sums_ref[1:2, here] += jnp.sum(g, 0, keepdims=True)
        split_rows(core_ref[0], value_s, kept_ref, sent_ref, here, None)

    pipelined(starts(width), product, scale)


def token_specs(planes, per_chip, rows, width, group):
    full = planes // group
    piece = pl.BlockSpec((group, 1, rows, width), lambda s, p, core: (p, s, 0, 0))

    def block(cols):
        return pl.BlockSpec((2 * group * rows, cols), lambda s, p, core: (s * full + p, 0))

    return (per_chip, full), piece, block


def pull_two(core, d, shared, normed, gain, h_one, planes, per_chip, rows):
    count, inner = d.shape
    width = gain.shape[1]
    group = math.gcd(planes, 2)
    grid, piece, block = token_specs(planes, per_chip, rows, width, group)
    low, high, _ = shared_specs(shared)
    shape = (planes, per_chip, rows, width)
    return pl.pallas_call(
        g_two_kernel,
        out_shape=(
            jax.ShapeDtypeStruct(shape, F32),
            jax.ShapeDtypeStruct(shape, BF),
            jax.ShapeDtypeStruct((2, width), F32),
        ),
        grid_spec=pltpu.PrefetchScalarGridSpec(
            num_scalar_prefetch=1,
            grid=grid,
            in_specs=[
                block(inner),
                low,
                high,
                block(width),
                pl.BlockSpec((1, width), lambda s, p, core: (0, 0)),
                block(width),
            ],
            out_specs=(piece, piece, pl.BlockSpec((2, width), lambda s, p, core: (0, 0))),
            scratch_shapes=[pltpu.VMEM((2 * group * rows, math.gcd(width, 512)), F32)],
        ),
        cost_estimate=pl.CostEstimate(
            flops=2 * count * width * inner,
            bytes_accessed=2 * count * (inner + 4 * width),
            transcendentals=0,
        ),
        compiler_params=pltpu.CompilerParams(vmem_limit_bytes=60 << 20),
    )(core.reshape(1), d, shared, shared, normed, gain, h_one)


def out_kernel(
    core_ref, z_ref, down_ref, attended_ref, x_ref, bias_ref, kept_ref, sent_ref, value_s
):
    def product(here):
        down = stacked(down_ref, slice(0, z_ref.shape[1]), here)
        return dot_nn(z_ref[...], down)

    def split(here, value):
        value_s[...] = value + attended_ref[:, here].astype(F32)
        split_rows(
            core_ref[0],
            value_s,
            kept_ref,
            sent_ref,
            here,
            lambda p: x_ref[p, 0, :, here].astype(F32) + bias_ref[:, here],
        )

    pipelined(starts(attended_ref.shape[1]), product, split)


def out_project(core, z, shared, attended, x_mine, bias, planes, per_chip, rows):
    count, hidden = z.shape
    width = attended.shape[1]
    group = math.gcd(planes, 2)
    grid, piece, block = token_specs(planes, per_chip, rows, width, group)
    shape = (planes, per_chip, rows, width)
    return pl.pallas_call(
        out_kernel,
        out_shape=(jax.ShapeDtypeStruct(shape, F32), jax.ShapeDtypeStruct(shape, BF)),
        grid_spec=pltpu.PrefetchScalarGridSpec(
            num_scalar_prefetch=1,
            grid=grid,
            in_specs=[
                block(hidden),
                shared_specs(shared)[2],
                block(width),
                piece,
                pl.BlockSpec((1, width), lambda s, p, core: (0, 0)),
            ],
            out_specs=(piece, piece),
            scratch_shapes=[pltpu.VMEM((2 * group * rows, math.gcd(width, 512)), F32)],
        ),
        cost_estimate=pl.CostEstimate(
            flops=2 * count * width * hidden,
            bytes_accessed=2 * count * (hidden + 5 * width),
            transcendentals=0,
        ),
        compiler_params=pltpu.CompilerParams(vmem_limit_bytes=60 << 20),
    )(core.reshape(1), z, shared, attended, x_mine.reshape(shape), bias)


def ordered(value, *before):
    return lax.optimization_barrier((value,) + before)[0]


def local(
    tokens,
    ln1_gain,
    ln1_shift,
    ln2_gain,
    ln2_shift,
    qkv_weight,
    qkv_bias,
    out_weight,
    out_bias,
    in_weight,
    in_bias,
    down_weight,
    down_bias,
    cotangent,
):
    planes = lax.axis_size("pl")
    chips = lax.axis_size("dp") * planes
    n = 2 * chips
    core = lax.axis_index("core")
    first_core = core == 0
    seqs, rows_here, width = tokens.shape
    per_chip = seqs // planes
    length = rows_here * planes * 2
    count = per_chip * length
    heads = H // 2
    qkv_cols = heads * 3 * HD
    ctx_cols = heads * HD
    hidden = in_weight.shape[1] // 2
    own_rows = qkv_weight.shape[0]

    def swap(value, mask):
        return lax.ppermute(value, AXES, [(i, i ^ mask) for i in range(n)])

    def in_core_order(own, other, axis):
        return jnp.where(
            first_core, jnp.concatenate([own, other], axis), jnp.concatenate([other, own], axis)
        )

    def pick(value, index, axis):
        return lax.dynamic_index_in_dim(value, index, axis, keepdims=False)

    qkv_halves = (
        qkv_weight.reshape(own_rows, 2, heads // 2, 2, 3, HD)
        .transpose(1, 0, 2, 4, 3, 5)
        .reshape(2, own_rows, qkv_cols)
    )
    out_halves = out_weight.reshape(own_rows, 2, ctx_cols).transpose(1, 0, 2)
    in_halves = (
        in_weight.reshape(own_rows, chips, 2, hidden // chips)
        .transpose(2, 0, 1, 3)
        .reshape(2, own_rows, hidden)
    )
    halves = jnp.concatenate([qkv_halves, out_halves, in_halves], 2)
    chip_rows = in_core_order(pick(halves, core, 0), swap(pick(halves, 1 - core, 0), 1), 0)
    first_cols = qkv_cols + ctx_cols
    first_all = lax.all_gather(chip_rows[:, :first_cols], CHIPS, axis=0, tiled=True)
    small = jnp.concatenate(
        [ln1_gain, ln1_shift, ln2_gain, ln2_shift, out_bias, down_bias, qkv_bias, in_bias]
    )
    small = jnp.broadcast_to(small[None, :], (n, small.shape[0]))
    small = ordered(small, chip_rows)
    small = lax.all_to_all(small, AXES, split_axis=0, concat_axis=0, tiled=True)
    small = small.astype(F32)
    part = width // n
    gain_one, shift_one, gain_two, shift_two, b_out, b_down = (
        small[:, i * part : (i + 1) * part].reshape(width) for i in range(6)
    )
    b_qkv = small[:, 6 * part : 9 * part].reshape(2, heads // 2, 2, 3, HD)
    b_qkv = pick(b_qkv, core, 0).transpose(0, 2, 1, 3).reshape(qkv_cols)
    b_in = pick(small[:, 9 * part :].reshape(chips, 2, hidden // chips), core, 1).reshape(hidden)

    deep = chips // planes
    second = jnp.concatenate(
        [
            chip_rows[:, first_cols : first_cols + width],
            chip_rows[:, first_cols + width :],
            down_weight,
        ],
        0,
    )
    shared = lax.all_gather(second[None], CHIPS, axis=0, tiled=True)
    other_rows = lax.dynamic_slice(first_all, ((1 - core) * ctx_cols, qkv_cols), (ctx_cols, ctx_cols))
    some_rows = lax.dynamic_slice(first_all, (core * ctx_cols, qkv_cols), (ctx_cols, ctx_cols))
    w_out = in_core_order(some_rows, swap(other_rows, 1), 1)
    w_qkv = first_all[:, :qkv_cols]

    def to_chip(value):
        mine = lax.all_to_all(value, "pl", split_axis=0, concat_axis=0, tiled=True)
        return mine, swap(mine, 1)

    def to_tokens(kept, sent):
        value = (kept + swap(sent, 1).astype(F32)).astype(BF)
        value = value.reshape(seqs, rows_here, width)
        return lax.all_to_all(value, "pl", split_axis=0, concat_axis=0, tiled=True)

    x_mine, x_theirs = to_chip(ordered(tokens, chip_rows))
    dy_mine, dy_theirs = to_chip(ordered(cotangent, x_mine))
    gains = jnp.stack([gain_one, shift_one, gain_two, shift_two])
    dy, dy_sum = on_pairs(dy_kernel, 1, core, dy_mine, dy_theirs, per_chip, sums=1)
    a_one, a_two, normed = on_pairs(
        norm_kernel, 3, core, x_mine, x_theirs, per_chip, (gains,)
    )

    qkv = (dot_nn(a_one, w_qkv) + b_qkv).astype(BF)
    context_grad = dot_nt(dy, w_out).astype(BF)
    context, qkv_grad = attention(
        qkv.reshape(per_chip, length, qkv_cols),
        context_grad.reshape(per_chip, length, ctx_cols),
        rotary_lanes(length),
    )
    context = context.reshape(count, ctx_cols)
    qkv_grad = qkv_grad.reshape(count, qkv_cols)

    plane_here = lax.axis_index("pl")
    deep_here = lax.axis_index("dp")

    def direct_sum(value, axis, size, here, stride, final):
        total = pick(value, here, axis).astype(F32)
        for k in range(1, size):
            total += swap(pick(value, here ^ k, axis), k * stride).astype(F32)
        return total if final else total.astype(BF)

    def plane_then_deep(value):
        value = value.reshape(deep, planes, value.shape[0] // chips, value.shape[1])
        value = direct_sum(value, 1, planes, plane_here, 2, False)
        return direct_sum(value, 0, deep, deep_here, 2 * planes, True)

    def deep_then_plane(value):
        value = value.reshape(deep, planes, value.shape[0] // chips, value.shape[1])
        value = direct_sum(value, 0, deep, deep_here, 2 * planes, False)
        return direct_sum(value, 0, planes, plane_here, 2, True)

    def own_rows_of(value):
        value = value.reshape(2, own_rows, value.shape[1])
        return pick(value, core, 0), swap(pick(value, 1 - core, 0), 1)

    out_w_grad = dot_tn(context, dy).astype(BF)
    other_cols = lax.dynamic_slice_in_dim(out_w_grad, (1 - core) * ctx_cols, ctx_cols, 1)
    own_cols = lax.dynamic_slice_in_dim(out_w_grad, core * ctx_cols, ctx_cols, 1)
    out_w_grad = in_core_order(own_cols, swap(other_cols, 1), 0)
    qkv_w_grad = dot_tn(a_one, qkv_grad).astype(BF)
    first_grad = jnp.concatenate([qkv_w_grad, out_w_grad], 1)
    first_grad = first_grad.reshape(deep, planes, 2 * own_rows, first_cols).transpose(1, 0, 2, 3)
    first_grad = lax.all_to_all(first_grad, "pl", split_axis=0, concat_axis=0, tiled=True)
    first_grad = jnp.sum(first_grad.astype(F32), 0).astype(BF)
    first_grad = direct_sum(first_grad, 0, deep, deep_here, 2 * planes, True)
    first_own, first_other = own_rows_of(first_grad)
    first_grad = in_core_order(first_own[:, None], first_other[:, None], 1)
    qkv_w_grad = (
        first_grad[:, :, :qkv_cols]
        .reshape(own_rows, 2, heads // 2, 3, 2, HD)
        .transpose(0, 1, 2, 4, 3, 5)
        .reshape(own_rows, 2 * qkv_cols)
    )
    out_w_grad = first_grad[:, :, qkv_cols:].reshape(own_rows, width)
    block = math.gcd(count, 512)
    h_one, sums_one, qkv_b_grad = pull_one(qkv_grad, first_all, normed, gain_one[None], block)

    qkv_b_grad = (
        qkv_b_grad.reshape(heads // 2, 3, 2, HD).transpose(0, 2, 1, 3).reshape(qkv_cols)
    )
    qkv_b_grad = in_core_order(qkv_b_grad, jnp.zeros_like(qkv_b_grad), 0)
    sums = [sums_one[0], sums_one[1], dy_sum, qkv_b_grad]
    sums = jnp.concatenate([value.reshape(n, -1) for value in sums], 1)
    sums = lax.all_to_all(sums, AXES, split_axis=0, concat_axis=0, tiled=True)
    sums = jnp.sum(sums, 0)

    attended = dot_nn(context, w_out).astype(BF)

    z, slope = up_project(a_two, shared, b_in[None], block)
    down_w_grad = dot_tn(z, dy).astype(BF)
    down_w_grad = plane_then_deep(down_w_grad)
    du, in_b_grad = down_pull(dy, shared, slope, block)
    in_w_grad = dot_tn(a_two, du).astype(BF)
    kept, sent, sums_two = pull_two(
        core, du, shared, normed, gain_two[None], h_one, planes, per_chip, rows_here
    )
    combined = to_tokens(kept, sent)
    per_row = hidden // width
    riders = jnp.concatenate(
        [sums_two.T, in_b_grad.reshape(width, per_row), jnp.zeros((width, PAIR - 2 - per_row), F32)], 1
    )
    in_w_grad = jnp.concatenate(
        [
            plane_then_deep(in_w_grad[:, : 15 * hidden // 16]),
            deep_then_plane(
                jnp.concatenate([in_w_grad[:, 15 * hidden // 16 :], riders.astype(BF)], 1)
            ),
        ],
        1,
    )
    in_b_grad = in_w_grad[:, hidden + 2 : hidden + 2 + per_row].reshape(hidden // chips)
    in_w_own, in_w_other = own_rows_of(in_w_grad)
    ln2_grads = (in_w_own + in_w_other)[:, hidden : hidden + 2]
    in_w_grad = weave(first_core, in_w_own, in_w_other, chips, hidden)
    kept, sent = out_project(
        core, z, shared, attended, x_mine, (b_out + b_down)[None], planes, per_chip, rows_here
    )
    output = to_tokens(kept, sent)

    x_here = tokens.astype(F32)
    mean_here = jnp.mean(x_here, axis=-1, keepdims=True)
    centred_here = x_here - mean_here
    scale_here = lax.rsqrt(jnp.mean(centred_here * centred_here, axis=-1, keepdims=True) + epsilon)
    normed_here = centred_here * scale_here
    combined = combined.astype(F32)
    pulled = (
        combined
        - jnp.mean(combined, axis=-1, keepdims=True)
        - normed_here * jnp.mean(combined * normed_here, axis=-1, keepdims=True)
    ) * scale_here
    dy_here = cotangent.astype(F32)
    input_grad = dy_here + pulled

    b_grad = sums[2 * part : 3 * part]
    return (
        output,
        input_grad,
        sums[:part],
        sums[part : 2 * part],
        ln2_grads[:, 0],
        ln2_grads[:, 1],
        qkv_w_grad,
        sums[3 * part :],
        out_w_grad,
        b_grad,
        in_w_grad,
        in_b_grad,
        down_w_grad,
        b_grad,
    )


def solution(mesh):
    split = Mesh(
        mesh.devices.reshape(mesh.shape["dp"], mesh.shape["seq"] // 2, 2),
        AXES,
    )
    rows = P("dp", ("pl", "core"), None)
    vector = P(AXES)
    matrix = P(AXES, None)
    return jax.shard_map(
        local,
        mesh=split,
        in_specs=(
            rows,
            vector,
            vector,
            vector,
            vector,
            matrix,
            vector,
            matrix,
            vector,
            matrix,
            vector,
            matrix,
            vector,
            rows,
        ),
        out_specs=(
            rows,
            rows,
            vector,
            vector,
            vector,
            vector,
            matrix,
            vector,
            matrix,
            vector,
            matrix,
            vector,
            matrix,
            vector,
        ),
        check_vma=False,
    )
```
